32 devices in a mesh: dp: 8 (over z, y), seq: 4 (over x, core).
Axes of the slice: x: 2, y: 2, z: 4, core: 2. Of those that a mesh axis runs over, the one named last changes fastest.
Arguments:
- inputs: float32 [8, 1024, 768], P('dp', 'seq'), may hold values from -40 to 40
- out_grad: float32 [8, 1024, 768], P('dp', 'seq'), may hold values from -6 to 6
- segment_ids: int32 [8, 1024], P('dp'), may hold values from 0 to 3, never falling along the last dimension, each value on 1 to 512 neighbouring positions
- params: float32 [3768320], P(('dp', 'seq')), may hold values from -7 to 2, as said below
- moment_one: float32 [3768320], P(('dp', 'seq')), may hold values from -28 to 28
- moment_two: float32 [3768320], P(('dp', 'seq')), may hold values from 40.96 to 409.6
Outputs:
- activations: float32 [8, 1024, 768], P('dp', 'seq')
- input_grad: float32 [8, 1024, 768], P('dp', 'seq')
- grad_flat: float32 [3768320], P(('dp', 'seq'))
- new_params: float32 [3768320], P(('dp', 'seq'))
- new_moment_one: float32 [3768320], P(('dp', 'seq'))
- new_moment_two: float32 [3768320], P(('dp', 'seq'))
The draws below stay inside these ranges and needn't reach their ends.
Inputs may be any that keep to these rules, and one draw needn't show every extreme that they name: segment_ids number the documents of each packed sequence from 0; they never fall along a sequence, each document holds 1 to 512 tokens and one holds exactly 512. The entries of params after the first 3765320 are zero.
All inputs are finite; a program needn't handle non-finite values.
Results may differ from the reference program's by a relative error of at most 0.011.
The reference program's roundings to bfloat16 on the way count: a program that leaves them out, or rounds other values in their place, can miss the bound.
Values may be sent and summed in bfloat16 or wider, within the bound.
No kernel may reach another device: no remote copies, remote signals or barrier semaphores. Data moves between devices by JAX's collectives and lax.ppermute only.
A program may use at most 128 MiB of HBM per device.

```python
import math
from functools import partial
import jax
import jax.numpy as jnp
import numpy as np
from jax import lax

D = 768
HEADS = 24
HEAD_DIM = 64
STATE = 128
KERNEL = 4
BLOCK = 256
INNER = 1536
PROJ = 3352
CONV_WIDTH = 1792
SEQS = 8
SEQ_LEN = 1024
TOKENS = 8192
DOCS = 4
DOC_MOST = 512
PARAMS = 3765320
FLAT = 3768320


def unit_noise(key, dims):
    return jnp.clip(jax.random.normal(key, dims, jnp.float32), -4.0, 4.0)


def draw_params(key, part):
    keys = jax.random.split(jax.random.fold_in(key, 11), 9)
    in_weight = unit_noise(keys[0], (D * PROJ,)) * D ** (-0.5)
    out_weight = unit_noise(keys[1], (INNER * D,)) * INNER ** (-0.5)
    conv_weight = unit_noise(keys[2], (KERNEL * CONV_WIDTH,)) * 0.5
    conv_bias = jax.random.uniform(keys[3], (CONV_WIDTH,), jnp.float32, -0.5, 0.5)
    norm_gain = jax.random.uniform(keys[4], (D,), jnp.float32, 0.5, 1.5)
    gated_gain = jax.random.uniform(keys[5], (INNER,), jnp.float32, 0.5, 1.5)
    delta_bias = jax.random.uniform(keys[6], (HEADS,), jnp.float32, -7.0, -3.0)
    decay_log = jax.random.uniform(keys[7], (HEADS,), jnp.float32, 0.0, 1.0)
    skip_gain = jax.random.uniform(keys[8], (HEADS,), jnp.float32, 0.5, 1.5)
    padding = jnp.zeros((FLAT - PARAMS,), jnp.float32)
    return jnp.concatenate([in_weight, out_weight, conv_weight, conv_bias, norm_gain, gated_gain, delta_bias, decay_log, skip_gain, padding])


def draw_inputs(key, part):
    keys = jax.random.split(jax.random.fold_in(key, 23), 3)
    noise = unit_noise(keys[0], (SEQS, SEQ_LEN, D))
    columns = jnp.exp(jax.random.uniform(keys[1], (D,), jnp.float32, -1.2039728, 1.0986123))
    row_scale = jnp.exp(jax.random.uniform(keys[2], (SEQS, SEQ_LEN, 1), jnp.float32, -1.0, 1.0))
    return noise * columns * row_scale


def block_levels(rng, shape, shards, low, high):
    level, own = 1.0, jax.random.fold_in(rng, 6)
    for dim, shards_of in shards:
        draws = jnp.exp(jax.random.uniform(jax.random.fold_in(own, dim), (shards_of,), jnp.float32, low / len(shards), high / len(shards)))
        level = level * jnp.repeat(draws, shape[dim] // shards_of).reshape([-1 if axis == dim else 1 for axis in range(len(shape))])
    return level


def length_profile(number_of, total, most, skew):
    weights = [(1 << 20) // math.isqrt(standing ** skew) + 1 for standing in range(2, number_of + 1)]
    rest, counts = total - most - (number_of - 1), [1] * (number_of - 1)
    while rest > 0:
        movable = [i for i in range(number_of - 1) if counts[i] < most]
        pool, left = sum([weights[i] for i in movable]), rest
        for i in movable:
            more = min(most - counts[i], max(1, left * weights[i] // pool), rest)
            counts[i] = counts[i] + more
            rest = rest - more
    return np.array([most] + counts)


def ragged(rng, number_of, total, reach, skew):
    if number_of == 2:
        one = jax.random.randint(rng, (), max(1, total - reach), min(reach, total - 1) + 1)
        return jnp.stack([one, total - one])
    lengths = jnp.asarray(length_profile(number_of, total, reach, skew), jnp.int32)
    twos = (number_of - 1) // 2
    giver, sink = lengths[1:1 + 2 * twos:2], lengths[2:2 + 2 * twos:2]
    room = jnp.minimum(giver - 1, reach - sink)
    moved = jax.random.randint(jax.random.fold_in(rng, 1), (twos,), 0, 1 << 20) % (room + 1)
    lengths = lengths.at[1:1 + 2 * twos:2].set(giver - moved).at[2:2 + 2 * twos:2].set(sink + moved)
    return lengths[jax.random.permutation(jax.random.fold_in(rng, 2), number_of)]


def bell_draw(key, shape, deviation, bound, cuts=(), held_as=jnp.bfloat16):
    entries = deviation * jax.random.normal(key, shape, jnp.float32)
    if cuts:
        entries = entries * block_levels(key, shape, cuts, -0.22, 0.18)
    return jnp.clip(entries, -bound, bound).astype(held_as)


def setup_inputs(seed: int = 0) -> dict:
    key_list = jax.random.split(jax.random.key(seed), 7)
    return {
        "inputs": draw_inputs(jax.random.fold_in(key_list[6], 71), 0),
        "out_grad": bell_draw(key_list[1], (SEQS, SEQ_LEN, D), 1.0, 6.0, ((0, 8), (1, 4)), jnp.float32),
        "segment_ids": jax.vmap(lambda own: jnp.searchsorted(jnp.cumsum(ragged(own, DOCS, SEQ_LEN, DOC_MOST, 2)), jnp.arange(SEQ_LEN), side="right"))(jax.random.split(key_list[2], SEQS)).reshape((SEQS, SEQ_LEN)).astype(jnp.int32),
        "params": draw_params(jax.random.fold_in(key_list[6], 71), 0),
        "moment_one": bell_draw(key_list[4], (FLAT,), (0.05 * TOKENS ** 0.5), 28.0, ((0, 32),), jnp.float32),
        "moment_two": jnp.clip(jnp.exp(math.log(409.6) - 2.3025851 * jax.random.uniform(key_list[5], (FLAT,), jnp.float32) ** block_levels(key_list[5], (FLAT,), ((0, 32),), -0.2, 0.2)), 40.96, 409.6),
    }


NORM_EPS = 1e-05
BETA_ONE = 0.9
BETA_TWO = 0.95
LEARN_RATE = 0.02
WEIGHT_DECAY = 0.1
ADAM_EPS = 1e-08
CORRECT_ONE = 1.0 - BETA_ONE ** 2
CORRECT_TWO = 1.0 - BETA_TWO ** 2
FULL_PRECISION = lax.Precision.HIGHEST

def layout_sizes():
    return [D * PROJ, INNER * D, KERNEL * CONV_WIDTH, CONV_WIDTH, D, INNER, HEADS, HEADS, HEADS]

def unpack(flat):
    pieces = []
    offset = 0
    for amount in layout_sizes():
        pieces.append(flat[offset:offset + amount])
        offset = offset + amount
    in_weight = pieces[0].reshape(D, PROJ)
    out_weight = pieces[1].reshape(INNER, D)
    conv_weight = pieces[2].reshape(KERNEL, CONV_WIDTH).astype(jnp.float32)
    vectors = [piece.astype(jnp.float32) for piece in pieces[3:]]
    return (in_weight, out_weight, conv_weight, vectors)

def front_norm(residual, gain):
    inv_rms = lax.rsqrt(lax.optimization_barrier(jnp.mean(residual * residual, axis=-1, keepdims=True)) + NORM_EPS)
    return residual * inv_rms * gain

def conv_mix(xbc_part, conv_weight, conv_bias, segments):
    length = xbc_part.shape[0]
    conv_out = conv_bias + conv_weight[KERNEL - 1] * xbc_part
    for distance in range(1, KERNEL):
        shifted = jnp.concatenate([jnp.zeros((distance, CONV_WIDTH), jnp.float32), xbc_part[:length - distance]], axis=0)
        earlier = jnp.concatenate([jnp.full((distance,), -1, jnp.int32), segments[:length - distance]])
        same_mask = (earlier == segments).astype(jnp.float32)[:, None]
        conv_out = conv_out + conv_weight[KERNEL - 1 - distance] * shifted * same_mask
    return conv_out

def state_space(values, b_proj, c_proj, step_size, log_decay, segments):
    length = values.shape[0]
    blocks = length // BLOCK
    values = values.reshape(blocks, BLOCK, HEADS, HEAD_DIM)
    b_proj = b_proj.reshape(blocks, BLOCK, STATE)
    c_proj = c_proj.reshape(blocks, BLOCK, STATE)
    step_size = step_size.reshape(blocks, BLOCK, HEADS)
    decay_sums = jnp.cumsum(log_decay.reshape(blocks, BLOCK, HEADS), axis=1)
    seg_blocks = segments.reshape(blocks, BLOCK)
    last_ids = seg_blocks[:, BLOCK - 1]
    prior_ids = jnp.concatenate([jnp.full((1,), -1, jnp.int32), last_ids[:blocks - 1]])
    row_index = lax.broadcasted_iota(jnp.int32, (BLOCK, BLOCK), 0)
    col_index = lax.broadcasted_iota(jnp.int32, (BLOCK, BLOCK), 1)
    allowed = (seg_blocks[:, :, None] == seg_blocks[:, None, :]) & (row_index >= col_index)[None]
    spread = jnp.transpose(decay_sums, (0, 2, 1))
    gap_sums = spread[:, :, :, None] - spread[:, :, None, :]
    decay_mask = jnp.exp(jnp.where(allowed[:, None], gap_sums, -jnp.inf))
    scores = jnp.einsum('kin,kjn->kij', c_proj, b_proj, precision=FULL_PRECISION)
    weighted = decay_mask * scores[:, None]
    scaled = values * step_size[..., None]
    inner_out = jnp.einsum('khij,kjhp->kihp', weighted, scaled, precision=FULL_PRECISION)
    tail_decay = jnp.where(seg_blocks[:, :, None] == last_ids[:, None, None], jnp.exp(decay_sums[:, BLOCK - 1:, :] - decay_sums), 0.0)
    local_state = jnp.einsum('kjhp,kjn->khpn', tail_decay[..., None] * scaled, b_proj, precision=FULL_PRECISION)
    carry_mult = jnp.exp(decay_sums[:, BLOCK - 1, :]) * (last_ids == prior_ids).astype(jnp.float32)[:, None]

    def advance(state_now, inputs_pair):
        factor, update = inputs_pair
        return (factor[:, None, None] * state_now + update, state_now)
    _, entering = lax.scan(advance, jnp.zeros((HEADS, HEAD_DIM, STATE), jnp.float32), (carry_mult, local_state))
    head_in = jnp.where(seg_blocks[:, :, None] == prior_ids[:, None, None], jnp.exp(decay_sums), 0.0)
    outer_out = jnp.einsum('kqn,khpn->kqhp', c_proj, entering, precision=FULL_PRECISION) * head_in[..., None]
    return (inner_out + outer_out).reshape(length, HEADS, HEAD_DIM)

def mixer(projected, conv_weight, conv_bias, delta_bias, decay_log, skip_gain, gated_gain, segments):
    length = projected.shape[0]
    gate_part = projected[:, :INNER]
    xbc_part = projected[:, INNER:INNER + CONV_WIDTH]
    raw_delta = projected[:, INNER + CONV_WIDTH:]
    conv_out = conv_mix(xbc_part, conv_weight, conv_bias, segments)
    active = jax.nn.silu(conv_out)
    values = active[:, :INNER].reshape(length, HEADS, HEAD_DIM)
    b_proj = active[:, INNER:INNER + STATE]
    c_proj = active[:, INNER + STATE:]
    step_size = jax.nn.softplus(raw_delta + delta_bias)
    log_decay = -step_size * jnp.exp(decay_log)
    ssd_out = state_space(values, b_proj, c_proj, step_size, log_decay, segments) + skip_gain[:, None] * values
    mixed_out = ssd_out.reshape(length, INNER) * jax.nn.silu(gate_part)
    norm_scale = lax.rsqrt(lax.optimization_barrier(jnp.mean(mixed_out * mixed_out, axis=-1, keepdims=True)) + NORM_EPS)
    return mixed_out * norm_scale * gated_gain

def reference(inputs, out_grad, segment_ids, params, moment_one, moment_two):
    narrow = params.astype(jnp.bfloat16)
    in_weight, out_weight, conv_weight, vectors = unpack(narrow)
    conv_bias, norm_gain, gated_gain, delta_bias, decay_log, skip_gain = vectors

    def per_sequence(totals, batch):
        residual, cotangent, segments = batch
        normed, front_back = jax.vjp(front_norm, residual, norm_gain)
        normed_narrow = normed.astype(jnp.bfloat16)
        projected = jnp.dot(normed_narrow, in_weight, preferred_element_type=jnp.float32).astype(jnp.bfloat16)
        projected = lax.optimization_barrier(projected).astype(jnp.float32)
        gated, middle_back = jax.vjp(partial(mixer, segments=segments), projected, conv_weight, conv_bias, delta_bias, decay_log, skip_gain, gated_gain)
        gated_narrow = gated.astype(jnp.bfloat16)
        activation = residual + jnp.dot(gated_narrow, out_weight, preferred_element_type=jnp.float32)
        cot_narrow = cotangent.astype(jnp.bfloat16)
        d_gated = jnp.dot(cot_narrow, out_weight.T, preferred_element_type=jnp.float32)
        grad_out = jnp.dot(gated_narrow.T, cot_narrow, preferred_element_type=jnp.float32)
        d_proj, grad_cw, grad_cb, grad_db, grad_dl, grad_skip, grad_gg = middle_back(d_gated)
        d_narrow = d_proj.astype(jnp.bfloat16)
        d_normed = jnp.dot(d_narrow, in_weight.T, preferred_element_type=jnp.float32)
        grad_in = jnp.dot(normed_narrow.T, d_narrow, preferred_element_type=jnp.float32)
        d_front, grad_ng = front_back(d_normed)
        gradient = cotangent + d_front
        pieces = (grad_in, grad_out, grad_cw, grad_cb, grad_ng, grad_gg, grad_db, grad_dl, grad_skip)
        totals = tuple((summed + piece for summed, piece in zip(totals, pieces)))
        return (totals, (activation, gradient))
    starting = (jnp.zeros((D, PROJ), jnp.float32), jnp.zeros((INNER, D), jnp.float32), jnp.zeros((KERNEL, CONV_WIDTH), jnp.float32), jnp.zeros((CONV_WIDTH,), jnp.float32), jnp.zeros((D,), jnp.float32), jnp.zeros((INNER,), jnp.float32), jnp.zeros((HEADS,), jnp.float32), jnp.zeros((HEADS,), jnp.float32), jnp.zeros((HEADS,), jnp.float32))
    totals, (activations, input_grad) = lax.scan(per_sequence, starting, (inputs, out_grad, segment_ids))
    grad_flat = jnp.concatenate([piece.reshape(-1) for piece in totals] + [jnp.zeros((params.shape[0] - PARAMS,), jnp.float32)])
    new_moment_one = BETA_ONE * moment_one + (1.0 - BETA_ONE) * grad_flat
    new_moment_two = BETA_TWO * moment_two + (1.0 - BETA_TWO) * grad_flat * grad_flat
    new_params = params - LEARN_RATE * (new_moment_one / CORRECT_ONE / (jnp.sqrt(new_moment_two / CORRECT_TWO) + ADAM_EPS) + WEIGHT_DECAY * params)
    return (activations, input_grad, grad_flat, new_params, new_moment_one, new_moment_two)
```

```python
import functools

import jax
import jax.numpy as jnp
import numpy as np
from jax import lax
from jax.experimental import pallas as pl
from jax.experimental.pallas import tpu as pltpu
from jax.sharding import PartitionSpec as P

D = 768
HEADS = 24
HEAD_DIM = 64
STATE = 128
KERNEL = 4
INNER = 1536
PROJ = 3352

NORM_EPS = 1e-05
BETA_ONE = 0.9
BETA_TWO = 0.95
LEARN_RATE = 0.02
WEIGHT_DECAY = 0.1
ADAM_EPS = 1e-08
CORRECT_ONE = 1.0 - BETA_ONE**2
CORRECT_TWO = 1.0 - BETA_TWO**2

LANES = 128
CHUNK = 128
GROUP = 4
OWN = INNER // GROUP
OWN_SLABS = OWN // LANES
MIXED = OWN + 2 * STATE
WIDE = 2 * OWN + 2 * STATE + LANES
SLABS = WIDE // LANES
HEADS_OWN = HEADS // GROUP
IN_SIZE = D * PROJ
OUT_END = IN_SIZE + INNER * D
ROW_SLABS = 32
OUT_SLABS = D // LANES
FRAME = HEAD_DIM * OUT_SLABS
SMALL = 48
PAD = FRAME + 16
MIB = 1024 * 1024

F32 = jnp.float32
BF16 = jnp.bfloat16


def up(value, step):
    return -(-value // step) * step


class Plan:
    def __init__(self, dp, seq, length):
        self.dp, self.seq, self.length = dp, seq, length
        count = dp * seq
        self.count = count
        self.first_out = IN_SIZE // length
        assert seq == GROUP and dp % 2 == 0 and length % LANES == 0
        assert IN_SIZE % length and (count - 1) * length <= OUT_END
        start = [i * length for i in range(count)]
        rows = []
        for i in range(self.first_out + 1):
            first = start[i] // PROJ
            last = (min(start[i] + length, IN_SIZE) - 1) // PROJ
            rows.append((first, last - first + 1))
        self.pure = up(max(n for _, n in rows[:-1]), 16)
        self.edge = up(rows[-1][1], 16)
        self.most_rows = max(n for _, n in rows)
        edge_out = -(-(start[self.first_out] + length - IN_SIZE) // D)
        assert edge_out <= HEAD_DIM
        self.edge_out = up(edge_out, 8)
        self.edge_at = SLABS * self.edge
        self.small_row = (OUT_END - start[-1]) // LANES
        self.pads = [self.pure] * self.first_out + [self.edge]
        self.offsets = [int(v) for v in np.cumsum([0] + self.pads[:-1])]
        self.depth = int(sum(self.pads))
        row_map = np.full((1, self.depth), -1, np.int32)
        for (first, n), at in zip(rows, self.offsets):
            row_map[0, at : at + n] = np.arange(first, first + n)
        self.row_map = row_map
        place = np.zeros((count, GROUP), np.int32)
        for i in range(self.first_out, count):
            low = max(start[i] - IN_SIZE, 0) // D // HEAD_DIM
            high = (min(start[i] + length, OUT_END) - 1 - IN_SIZE) // D // HEAD_DIM
            assert high - low < GROUP
            for head in range(low, high + 1):
                place[i, head % GROUP] = head // GROUP
        self.place = place
        self.frame_rows = HEAD_DIM if length > D * HEAD_DIM else up(length // D + 2, 8)
        if self.frame_rows < HEAD_DIM:
            for i in range(self.first_out, count):
                for rank in range(GROUP):
                    begin = max(start[i] - IN_SIZE, 0) // D
                    head = self.place[i, rank] * GROUP + rank
                    self.place[i, rank] = self.place[i, rank] * HEAD_DIM + max(
                        begin - head * HEAD_DIM, 0
                    )
        else:
            self.place = self.place * HEAD_DIM
        self.frame = self.frame_rows * OUT_SLABS
        need = max(
            SLABS * self.pure, self.edge_at + OUT_SLABS * self.edge_out, self.frame + SMALL
        )
        self.block = up(need, 16)

    def scalars(self, index):
        begin = index * self.length
        first = begin // PROJ
        last = (jnp.minimum(begin + self.length, IN_SIZE) - 1) // PROJ
        form = jnp.where(index < self.first_out, 0, jnp.where(index == self.first_out, 1, 2))
        low = jnp.maximum(begin - IN_SIZE, 0) // D // HEAD_DIM
        high = (jnp.minimum(begin + self.length, OUT_END) - 1 - IN_SIZE) // D // HEAD_DIM
        values = [form, first * PROJ - begin, last - first + 1, index == self.count - 1]
        counts = []
        for rank in range(GROUP):
            head = low + (rank - low) % GROUP
            row = head * HEAD_DIM
            rows = HEAD_DIM
            if self.frame_rows < HEAD_DIM:
                top = jnp.maximum(begin - IN_SIZE, 0) // D
                bottom = (jnp.minimum(begin + self.length, OUT_END) - 1 - IN_SIZE) // D + 1
                rows = jnp.minimum(row + HEAD_DIM, bottom) - jnp.maximum(row, top)
                row = jnp.maximum(row, top)
            at = (IN_SIZE + row * D - begin) // LANES
            held = (head <= high) & (form > 0)
            values.append(jnp.where(held, at, -PAD))
            counts.append(jnp.where(held, rows * OUT_SLABS, 0))
        values += counts
        return jnp.stack([jnp.asarray(v, jnp.int32) for v in values])


def lane_iota(rows):
    return lax.broadcasted_iota(jnp.int32, (rows, LANES), 1)


def join_halves(first, second, rank):
    lane = lane_iota(first.shape[0])
    if rank % 2 == 0:
        return jnp.where(lane < 64, first, pltpu.roll(second, 64, 1))
    return jnp.where(lane < 64, pltpu.roll(first, 64, 1), second)


def own_slab(get, rank, slab):
    return join_halves(get(4 * slab + rank // 2), get(4 * slab + 2 + rank // 2), rank)


def whole_slab(get, slab):
    half = (slab // 2) % 2
    return join_halves(get((2 * slab) % 4, slab // 4), get((2 * slab + 1) % 4, slab // 4), half)


def pack_kernel(plan, sc, x_ref, out_ref, flat, rowbuf, frame, small):
    local = x_ref.shape[0]
    flat[...] = jnp.zeros_like(flat)
    flat[PAD : PAD + local, :] = x_ref[...]
    out_ref[...] = jnp.zeros_like(out_ref)
    lane = lane_iota(ROW_SLABS)
    form = sc[0]

    @pl.when(form < 2)
    def _():
        rowbuf[...] = jnp.zeros_like(rowbuf)

        def row(r, carry):
            at = sc[1] + r * PROJ + PAD * LANES
            sub, shift = at // LANES, at % LANES
            turn = (LANES - shift) % LANES
            near = pltpu.roll(flat[pl.ds(sub, ROW_SLABS), :], turn, 1)
            far = pltpu.roll(flat[pl.ds(sub + 1, ROW_SLABS), :], turn, 1)
            joined = jnp.where(lane < LANES - shift, near, far)
            rowbuf[pl.ds(pl.multiple_of(r * ROW_SLABS, ROW_SLABS), ROW_SLABS), :] = jnp.where(
                r < sc[2], joined, 0.0
            )
            return carry

        lax.fori_loop(0, plan.most_rows, row, 0)

    def weights(depth):
        def get(column):
            return rowbuf[pl.ds(column, depth, stride=ROW_SLABS), :]

        for rank in range(GROUP):
            slabs = [own_slab(get, rank, m) for m in range(OWN_SLABS)]
            slabs += [own_slab(lambda c: get(12 + c), rank, m) for m in range(OWN_SLABS)]
            slabs += [get(24), get(25), jnp.where(lane_iota(depth) < HEADS, get(26), 0.0)]
            for j, slab in enumerate(slabs):
                out_ref[rank, j * depth : (j + 1) * depth, :] = slab.astype(BF16)

    @pl.when(form == 0)
    def _():
        weights(plan.pure)

    @pl.when(form == 1)
    def _():
        weights(plan.edge)

    def frames(rows, base):
        for rank in range(GROUP):
            row = lax.broadcasted_iota(jnp.int32, (plan.frame, LANES), 0)
            frame[...] = jnp.where(
                row < sc[8 + rank], flat[pl.ds(sc[4 + rank] + PAD, plan.frame), :], 0.0
            )
            for j in range(OUT_SLABS):
                out_ref[rank, base + j * rows : base + (j + 1) * rows, :] = frame[
                    pl.ds(j, rows, stride=OUT_SLABS), :
                ].astype(BF16)

    @pl.when(form == 1)
    def _():
        frames(plan.edge_out, plan.edge_at)

    @pl.when(form == 2)
    def _():
        frames(plan.frame_rows, 0)

    @pl.when(sc[3] == 1)
    def _():
        base = PAD + plan.small_row

        def get(row):
            return flat[base + row : base + row + 1, :]

        small[...] = jnp.zeros_like(small)
        for rank in range(GROUP):
            at = 0
            for k in range(KERNEL + 1):
                for m in range(OWN_SLABS):
                    small[at : at + 1, :] = own_slab(lambda c: get(14 * k + c), rank, m)
                    at += 1
                for row in (12, 13):
                    small[at : at + 1, :] = get(14 * k + row)
                    at += 1
            for row in range(70, 76):
                small[at : at + 1, :] = get(row)
                at += 1
            for m in range(OWN_SLABS):
                small[at : at + 1, :] = own_slab(lambda c: get(76 + c), rank, m)
                at += 1
            small[at : at + 1, :] = get(88)
            out_ref[rank, plan.frame : plan.frame + SMALL, :] = small[...].astype(BF16)


def unpack_kernel(
    plan, sc, blk, par, one, two, grad_ref, par_ref, one_ref, two_ref, flat, rowbuf, frame
):
    local = par.shape[0]
    flat[...] = jnp.zeros_like(flat)
    lane = lane_iota(ROW_SLABS)
    form = sc[0]

    def total(at, rows):
        parts = [blk[rank, at : at + rows, :].astype(F32) for rank in range(GROUP)]
        return (parts[0] + parts[1]) + (parts[2] + parts[3])

    def weights(depth):
        rowbuf[...] = jnp.zeros_like(rowbuf)

        def get(base):
            def piece(rank, m):
                at = (base + m) * depth
                return blk[rank, at : at + depth, :].astype(F32)

            return piece

        for half in range(2):
            for j in range(12):
                rowbuf[pl.ds(12 * half + j, depth, stride=ROW_SLABS), :] = whole_slab(
                    get(OWN_SLABS * half), j
                )
        for j in range(3):
            rowbuf[pl.ds(24 + j, depth, stride=ROW_SLABS), :] = total((6 + j) * depth, depth)

    def rows():
        def row(r, carry):
            at = sc[1] + r * PROJ + PAD * LANES
            sub, shift = at // LANES, at % LANES
            value = rowbuf[pl.ds(pl.multiple_of(r * ROW_SLABS, ROW_SLABS), ROW_SLABS), :]
            value = pltpu.roll(jnp.where(r < sc[2], value, 0.0), shift, 1)
            flat[pl.ds(sub, ROW_SLABS), :] += jnp.where(lane >= shift, value, 0.0)
            flat[pl.ds(sub + 1, ROW_SLABS), :] += jnp.where(lane < shift, value, 0.0)
            return carry

        lax.fori_loop(0, plan.most_rows, row, 0)

    def frames(count, base):
        for rank in range(GROUP):
            frame[...] = jnp.zeros_like(frame)
            for j in range(OUT_SLABS):
                frame[pl.ds(j, count, stride=OUT_SLABS), :] = blk[
                    rank, base + j * count : base + (j + 1) * count, :
                ].astype(F32)
            row = lax.broadcasted_iota(jnp.int32, (plan.frame, LANES), 0)
            flat[pl.ds(sc[4 + rank] + PAD, plan.frame), :] += jnp.where(
                row < sc[8 + rank], frame[...], 0.0
            )

    @pl.when(form == 0)
    def _():
        weights(plan.pure)
        rows()

    @pl.when(form == 1)
    def _():
        frames(plan.edge_out, plan.edge_at)
        weights(plan.edge)
        rows()

    @pl.when(form == 2)
    def _():
        frames(plan.frame_rows, 0)

    @pl.when(sc[3] == 1)
    def _():
        base = PAD + plan.small_row
        rows = [blk[rank, plan.frame : plan.frame + SMALL, :].astype(F32) for rank in range(GROUP)]
        summed = (rows[0] + rows[1]) + (rows[2] + rows[3])

        def get(start):
            return lambda rank, m: rows[rank][start + m : start + m + 1]

        for k in range(KERNEL + 1):
            at = base + 14 * k
            for j in range(12):
                flat[at + j : at + j + 1, :] = whole_slab(get(5 * k), j)
            flat[at + 12 : at + 14, :] = summed[5 * k + 3 : 5 * k + 5]
        flat[base + 70 : base + 76, :] = summed[25:31]
        for j in range(12):
            flat[base + 76 + j : base + 77 + j, :] = whole_slab(get(31), j)
        flat[base + 88 : base + 89, :] = summed[34:35]

    grad = flat[PAD : PAD + local, :]
    new_one = BETA_ONE * one[...] + (1.0 - BETA_ONE) * grad
    new_two = BETA_TWO * two[...] + (1.0 - BETA_TWO) * grad * grad
    params = par[...]
    grad_ref[...] = grad
    one_ref[...] = new_one
    two_ref[...] = new_two
    par_ref[...] = params - LEARN_RATE * (
        new_one / CORRECT_ONE / (jnp.sqrt(new_two / CORRECT_TWO) + ADAM_EPS)
        + WEIGHT_DECAY * params
    )


def mm(a, b):
    return lax.dot_general(a, b, (((1,), (0,)), ((), ())), preferred_element_type=F32)


def mm_nt(a, b):
    return lax.dot_general(a, b, (((1,), (1,)), ((), ())), preferred_element_type=F32)


def mm_tn(a, b):
    return lax.dot_general(a, b, (((0,), (0,)), ((), ())), preferred_element_type=F32)


def thirds(value):
    high = value.astype(BF16)
    rest = value - high.astype(F32)
    middle = rest.astype(BF16)
    return high, middle, (rest - middle.astype(F32)).astype(BF16)


def expand(value):
    rows = value.shape[0]
    lane = lane_iota(rows)
    return jnp.concatenate(
        [
            jnp.where(lane < 64, value[:, 8 * m : 8 * m + 1], value[:, 8 * m + 4 : 8 * m + 5])
            for m in range(OWN_SLABS)
        ],
        axis=1,
    )


def head_sums(value):
    row = lax.broadcasted_iota(jnp.int32, (OWN, LANES), 0)
    col = lax.broadcasted_iota(jnp.int32, (OWN, LANES), 1)
    pick = (col == GROUP * (row // HEAD_DIM)).astype(BF16)
    high = value.astype(BF16)
    low = (value - high.astype(F32)).astype(BF16)
    return mm(high, pick) + mm(low, pick)


def small_rows(small, start, count):
    return jnp.concatenate([small[start + m : start + m + 1, :] for m in range(count)], axis=1)


class Small:
    def __init__(self, small, rank):
        self.taps = [small_rows(small, 5 * k, 5) for k in range(KERNEL)]
        self.conv_bias = small_rows(small, 20, 5)
        self.gated_gain = small_rows(small, 31, OWN_SLABS)
        vec = small[34:35, :]
        lane = lane_iota(1)
        self.heads = (lane % GROUP == 0) & (lane < HEADS)

        def pick(at):
            turned = pltpu.roll(vec, (2 * LANES - at - rank) % LANES, 1)
            return jnp.where(self.heads, turned, 0.0)

        self.delta_bias = pick(0)
        self.rate = jnp.where(self.heads, -jnp.exp(pick(HEADS)), 0.0)
        self.skip = expand(pick(2 * HEADS))


def triangle(lower):
    row = lax.broadcasted_iota(jnp.int32, (CHUNK, CHUNK), 0)
    col = lax.broadcasted_iota(jnp.int32, (CHUNK, CHUNK), 1)
    return (row >= col) if lower else (row <= col)


class Front:
    def __init__(self, c, rank, sm, xf, proj, tok, segr):
        at = pl.multiple_of(c * CHUNK, CHUNK)
        window = xf[pl.ds(at, CHUNK + 8), :]
        self.shifted = [window[8 - d : 8 - d + CHUNK] for d in range(KERNEL)]
        tk = tok[pl.ds(at, CHUNK), :]
        self.masks = [None] + [tk[:, d : d + 1] for d in range(1, KERNEL)]
        conv = sm.conv_bias + sm.taps[KERNEL - 1] * self.shifted[0]
        for d in range(1, KERNEL):
            conv = conv + sm.taps[KERNEL - 1 - d] * self.shifted[d] * self.masks[d]
        self.conv = conv
        self.conv_sig = jax.nn.sigmoid(conv)
        act = conv * self.conv_sig
        self.values = act[:, :OWN]
        self.b = act[:, OWN : OWN + STATE].astype(BF16)
        self.c = act[:, OWN + STATE :].astype(BF16)
        raw = proj[pl.ds(at, CHUNK), WIDE - LANES :].astype(F32)
        pre = pltpu.roll(raw, (LANES - rank) % LANES, 1) + sm.delta_bias
        self.pre = pre
        self.step = jnp.where(
            sm.heads, jnp.maximum(pre, 0.0) + jnp.log1p(jnp.exp(-jnp.abs(pre))), 0.0
        )
        log_decay = self.step * sm.rate
        lower = triangle(True)
        ones = lower.astype(BF16)
        high, middle, low = thirds(log_decay)
        sums = mm(ones, high) + (mm(ones, middle) + mm(ones, low))
        self.sums = sums
        self.sums_t = sums.T
        last = sums[CHUNK - 1 : CHUNK, :]
        self.allowed = (tk[:, 0:1] == segr[pl.ds(c, 1), :]) & lower
        self.step_wide = expand(self.step)
        self.scaled = self.values * self.step_wide
        self.scaled_n = self.scaled.astype(BF16)
        self.head_in = expand(jnp.exp(sums) * tk[:, 4:5])
        self.tail = expand(jnp.exp(last - sums) * tk[:, 5:6])
        self.carry = expand(jnp.exp(last) * tk[CHUNK - 1 : CHUNK, 6:7])
        self.tail_scaled = self.tail * self.scaled
        self.scores = mm_nt(self.c, self.b)
        gate = proj[pl.ds(at, CHUNK), :OWN].astype(F32)
        self.gate = gate
        self.gate_sig = jax.nn.sigmoid(gate)
        self.gate_act = gate * self.gate_sig

    def decay(self, k):
        gap = self.sums[:, 4 * k : 4 * k + 1] - self.sums_t[4 * k : 4 * k + 1, :]
        return jnp.exp(jnp.where(self.allowed, gap, -1e30))

    def head(self, value, k):
        return value[:, HEAD_DIM * k : HEAD_DIM * (k + 1)]


def fill_xf(xf, proj, tokens):
    xf[0:8, :] = jnp.zeros((8, MIXED), F32)
    xf[8 : 8 + tokens, :] = proj[:, OWN : OWN + MIXED].astype(F32)


def forward_kernel(plan, place, sc, row_map, tok, segr, *refs):
    dp = plan.dp
    x_in, c_in, w_in = refs[:4], refs[4:8], refs[8 : 8 + dp]
    refs = refs[8 + dp :]
    (proj, ssd, d_gated, states, sums_ref, w_sf, w_out, small_ref, spread, x_hat, cots) = refs[:11]
    xs, blocks, w_acc, xf, state, sem = refs[11:]
    tokens = xs.shape[0]
    piece = tokens // GROUP
    rank, group = sc[0], sc[1]
    line = dp // 2
    copies = []
    for j in range(dp):
        where = lax.rem(group // 2 + line - j // 2, line) * 2 + lax.rem(group + j % 2, 2)
        copies.append(pltpu.make_async_copy(w_in[j], blocks.at[where], sem.at[j]))
    for r in range(GROUP):
        at = pl.multiple_of((rank ^ r) * piece, piece)
        copies.append(pltpu.make_async_copy(x_in[r], xs.at[pl.ds(at, piece)], sem.at[dp + r]))
        copies.append(
            pltpu.make_async_copy(c_in[r], cots.at[pl.ds(at, piece)], sem.at[dp + GROUP + r])
        )
    for copy in copies:
        copy.start()
    for copy in copies:
        copy.wait()

    def rows_of(i, at, depth):
        for j in range(SLABS):
            w_sf[pl.ds(at, depth), j * LANES : (j + 1) * LANES] = blocks[
                i // GROUP, i % GROUP, j * depth : (j + 1) * depth, :
            ]

    def pure_rows(i, carry):
        rows_of(i, pl.multiple_of(i * plan.pure, plan.pure), plan.pure)
        return carry

    lax.fori_loop(0, plan.first_out, pure_rows, 0)
    rows_of(plan.first_out, plan.offsets[-1], plan.edge)
    w_acc[...] = jnp.zeros_like(w_acc)
    for i in range(plan.first_out, plan.count):
        rows, base = (plan.edge_out, plan.edge_at) if i == plan.first_out else (plan.frame_rows, 0)
        at = place[i * GROUP + rank]
        if plan.frame_rows == HEAD_DIM:
            at = pl.multiple_of(at, HEAD_DIM)
        for j in range(OUT_SLABS):
            w_acc[j, pl.ds(at, rows), :] += blocks[
                i // GROUP, i % GROUP, base + j * rows : base + (j + 1) * rows, :
            ].astype(F32)
    for j in range(OUT_SLABS):
        w_out[:, j * LANES : (j + 1) * LANES] = w_acc[j, 0:OWN, :].astype(BF16)
    small = blocks[dp - 1, GROUP - 1, plan.frame : plan.frame + SMALL, :].astype(F32)
    small_ref[...] = small
    sm = Small(small, rank)
    norm_gain = small_rows(small, 25, OUT_SLABS)
    chosen = (
        lax.broadcasted_iota(jnp.int32, (D, plan.depth), 0) == row_map[...]
    ).astype(BF16)

    def tile(t, carry):
        at = pl.ds(pl.multiple_of(t * 256, 256), 256)
        x = xs[at, :]
        scale = lax.rsqrt(jnp.sum(x * x, axis=1, keepdims=True) * (1.0 / D) + NORM_EPS)
        unit = x * scale
        x_hat[at, :] = unit.astype(BF16)
        wide = mm((unit * norm_gain).astype(BF16), chosen).astype(BF16)
        spread[at, :] = wide
        proj[at, :] = mm(wide, w_sf[...]).astype(BF16)
        d_gated[at, :] = mm_nt(cots[at, :], w_out[...])
        return carry

    lax.fori_loop(0, tokens // 256, tile, 0)
    fill_xf(xf, proj, tokens)
    state[...] = jnp.zeros_like(state)

    def chunk(c, carry):
        at = pl.ds(pl.multiple_of(c * CHUNK, CHUNK), CHUNK)
        f = Front(c, rank, sm, xf, proj, tok, segr)
        inner = []
        for k in range(HEADS_OWN):
            weighted = (f.decay(k) * f.scores).astype(BF16)
            inner.append(mm(weighted, f.head(f.scaled_n, k)))
        entering = state[...]
        states[c] = entering
        through = mm(f.c, entering.astype(BF16))
        out = jnp.concatenate(inner, axis=1) + through * f.head_in + sm.skip * f.values
        ssd[at, :] = out
        state[...] = f.carry * entering + mm_tn(f.b, f.tail_scaled.astype(BF16))
        mixed = out * f.gate_act
        first = jnp.sum(mixed * mixed, axis=1, keepdims=True)
        second = jnp.sum(d_gated[at, :] * sm.gated_gain * mixed, axis=1, keepdims=True)
        both = jnp.where(lane_iota(CHUNK) == 0, first, second)
        sums_ref[:, at] = both.T[0:8, :]
        return carry

    lax.fori_loop(0, tokens // CHUNK, chunk, 0)


def fold(value):
    rows, width = value.shape
    return jnp.sum(value.reshape(rows // 8, 8, width), axis=0)


def backward_kernel(
    plan, place, sc, row_map, tok, segr, sums_ref, proj, ssd, d_gated, states, w_sf, w_out,
    small_ref, spread, x_hat, cots, *refs
):
    dp = plan.dp
    blocks_out, act_out, back_out = refs[:dp], refs[dp], refs[dp + 1]
    (blocks, xf, dcf, adjoint, gated, dn, colbuf, acc_gg, acc_skip, acc_conv, acc_head, acc_ng,
     wide_out, sem) = refs[dp + 2 :]
    tokens = proj.shape[0]
    piece = tokens // GROUP
    rank, group = sc[0], sc[1]
    chunks = tokens // CHUNK
    sm = Small(small_ref[...], rank)
    fill_xf(xf, proj, tokens)
    for ref in (dcf, adjoint, colbuf, acc_gg, acc_skip, acc_conv, acc_head, acc_ng):
        ref[...] = jnp.zeros_like(ref)
    lane = lane_iota(CHUNK)

    def chunk(i, carry):
        c = chunks - 1 - i
        start = pl.multiple_of(c * CHUNK, CHUNK)
        at = pl.ds(start, CHUNK)
        f = Front(c, rank, sm, xf, proj, tok, segr)
        both = jnp.concatenate([sums_ref[:, at]] * (CHUNK // 8), axis=0).T
        norm = lax.rsqrt(both[:, 0:1] * (1.0 / INNER) + NORM_EPS)
        drag = norm * (both[:, 1:2] * (1.0 / INNER))
        out = ssd[at, :]
        dg = d_gated[at, :]
        unit = out * f.gate_act * norm
        gated[at, :] = (unit * sm.gated_gain).astype(BF16)
        acc_gg[...] += fold(dg * unit)
        d_mixed = norm * (dg * sm.gated_gain - unit * drag)
        d_ssd = d_mixed * f.gate_act
        d_gate = d_mixed * out * (f.gate_sig * (1.0 + f.gate * (1.0 - f.gate_sig)))
        acc_skip[...] += fold(d_ssd * f.values)
        d_ssd_n = d_ssd.astype(BF16)
        entering = states[c]
        entering_n = entering.astype(BF16)
        leaving = adjoint[...]
        leaving_n = leaving.astype(BF16)
        head_ssd = f.head_in * d_ssd
        head_ssd_n = head_ssd.astype(BF16)
        through = mm(f.c, entering_n)
        exit_b = mm(f.b, leaving_n)
        tail_flow = f.tail_scaled * exit_b
        last_row = jnp.sum(tail_flow, axis=0, keepdims=True) + f.carry * jnp.sum(
            leaving * entering, axis=0, keepdims=True
        )
        row = lax.broadcasted_iota(jnp.int32, (CHUNK, OWN), 0)
        flow = head_ssd * through - tail_flow + jnp.where(row == CHUNK - 1, last_row, 0.0)
        d_scores = jnp.zeros((CHUNK, CHUNK), F32)
        d_scaled = []
        row_sums = jnp.zeros((CHUNK, LANES), F32)
        for k in range(HEADS_OWN):
            decay = f.decay(k)
            weighted = decay * f.scores
            d_head = f.head(d_ssd_n, k)
            d_weighted = mm_nt(d_head, f.head(f.scaled_n, k))
            d_scaled.append(mm_tn(weighted.astype(BF16), d_head))
            d_scores = d_scores + d_weighted * decay
            flows = d_weighted * weighted
            row_sums = jnp.where(lane == 4 * k, jnp.sum(flows, axis=1, keepdims=True), row_sums)
            colbuf[4 * k : 4 * k + 1, :] = jnp.sum(flows, axis=0, keepdims=True)
        d_scaled = jnp.concatenate(d_scaled, axis=1) + f.tail * exit_b
        d_scores_n = d_scores.astype(BF16)
        d_c = mm_nt(head_ssd_n, entering_n) + mm(d_scores_n, f.b)
        d_b = mm_tn(d_scores_n, f.c) + mm_nt(f.tail_scaled.astype(BF16), leaving_n)
        adjoint[...] = f.carry * leaving + mm_tn(f.c, head_ssd_n)
        d_sums = row_sums - colbuf[...].T + head_sums(flow)
        upper = triangle(False).astype(BF16)
        high, middle, low = thirds(d_sums)
        d_log = mm(upper, high) + (mm(upper, middle) + mm(upper, low))
        d_values = sm.skip * d_ssd + d_scaled * f.step_wide
        d_step = head_sums(d_scaled * f.values) + d_log * sm.rate
        d_raw = jnp.where(sm.heads, d_step * jax.nn.sigmoid(f.pre), 0.0)
        acc_head[0:8, :] += fold(d_raw)
        acc_head[8:16, :] += fold(d_log * f.step) * sm.rate
        d_act = jnp.concatenate([d_values, d_b, d_c], axis=1)
        d_conv = d_act * (f.conv_sig * (1.0 + f.conv * (1.0 - f.conv_sig)))
        acc_conv[8 * KERNEL : 8 * KERNEL + 8, :] += fold(d_conv)
        acc_conv[8 * (KERNEL - 1) : 8 * KERNEL, :] += fold(d_conv * f.shifted[0])
        for d in range(1, KERNEL):
            lower = 8 * (KERNEL - 1 - d)
            acc_conv[lower : lower + 8, :] += fold(d_conv * f.shifted[d] * f.masks[d])
        dcf[at, :] = d_conv
        window = dcf[pl.ds(start, CHUNK + 8), :]
        masks = tok[pl.ds(start, CHUNK + 8), :]
        d_x = sm.taps[KERNEL - 1] * d_conv
        for d in range(1, KERNEL):
            masked = window * masks[:, d : d + 1]
            d_x = d_x + sm.taps[KERNEL - 1 - d] * masked[d : d + CHUNK]
        dn[at, 0:OWN] = d_gate.astype(BF16)
        dn[at, OWN : OWN + MIXED] = d_x.astype(BF16)
        dn[at, WIDE - LANES :] = pltpu.roll(d_raw, rank, 1).astype(BF16)
        return carry

    lax.fori_loop(0, chunks, chunk, 0)
    chosen = (
        lax.broadcasted_iota(jnp.int32, (D, plan.depth), 0) == row_map[...]
    ).astype(BF16)

    for token_group in range(GROUP):
        rel = token_group ^ rank
        at = slice(token_group * piece, (token_group + 1) * piece)
        act_out[lax.rem(rel, 2), rel // 2] = mm(gated[at, :], w_out[...]).astype(BF16)
        wide = mm_nt(dn[at, :], w_sf[...]).astype(BF16)
        d_normed = mm_nt(wide, chosen)
        back_out[lax.rem(rel, 2), rel // 2] = d_normed.astype(BF16)
        acc_ng[...] += fold(d_normed * x_hat[at, :].astype(F32))

    line = dp // 2

    def slot(i):
        to = i // GROUP
        return lax.rem(to // 2 + line - group // 2, line) * 2 + (lax.rem(to + group, 2))

    span = SLABS if plan.depth <= 2048 else OWN_SLABS
    for first in range(0, SLABS, span):
        grad_in = mm_tn(spread[...], dn[:, first * LANES : (first + span) * LANES])
        for i in range(plan.first_out + 1):
            depth, at = plan.pads[i], plan.offsets[i]
            to = slot(i)
            for j in range(span):
                base = (first + j) * depth
                blocks[to, i % GROUP, base : base + depth, :] = grad_in[
                    at : at + depth, j * LANES : (j + 1) * LANES
                ].astype(BF16)
    grad_out = mm_tn(gated[...], cots[...])
    for j in range(OUT_SLABS):
        wide_out[j, 0:OWN, :] = grad_out[:, j * LANES : (j + 1) * LANES]
        wide_out[j, OWN:, :] = jnp.zeros((plan.frame_rows, LANES), F32)
    for i in range(plan.first_out, plan.count):
        rows, base = (plan.edge_out, plan.edge_at) if i == plan.first_out else (plan.frame_rows, 0)
        at = place[i * GROUP + rank]
        if plan.frame_rows == HEAD_DIM:
            at = pl.multiple_of(at, HEAD_DIM)
        to = slot(i)
        for j in range(OUT_SLABS):
            blocks[to, i % GROUP, base + j * rows : base + (j + 1) * rows, :] = wide_out[
                j, pl.ds(at, rows), :
            ].astype(BF16)
    tail = []
    for k in range(KERNEL + 1):
        line_sum = jnp.sum(acc_conv[8 * k : 8 * k + 8, :], axis=0, keepdims=True)
        tail += [line_sum[:, m * LANES : (m + 1) * LANES] for m in range(5)]
    gain = jnp.sum(acc_ng[...], axis=0, keepdims=True)
    tail += [gain[:, m * LANES : (m + 1) * LANES] for m in range(OUT_SLABS)]
    gain = jnp.sum(acc_gg[...], axis=0, keepdims=True)
    tail += [gain[:, m * LANES : (m + 1) * LANES] for m in range(OWN_SLABS)]
    bias = jnp.sum(acc_head[0:8, :], axis=0, keepdims=True)
    rate = jnp.sum(acc_head[8:16, :], axis=0, keepdims=True)
    skip = jnp.sum(head_sums(acc_skip[...]), axis=0, keepdims=True)
    heads = sm.heads
    vec = pltpu.roll(jnp.where(heads, bias, 0.0), rank, 1)
    vec = vec + pltpu.roll(jnp.where(heads, rate, 0.0), rank + HEADS, 1)
    vec = vec + pltpu.roll(jnp.where(heads, skip, 0.0), rank + 2 * HEADS, 1)
    tail += [vec, jnp.zeros((SMALL - len(tail) - 1, LANES), F32)]
    blocks[slot(plan.count - 1), GROUP - 1, plan.frame : plan.frame + SMALL, :] = jnp.concatenate(
        tail, axis=0
    ).astype(BF16)
    copies = [
        pltpu.make_async_copy(blocks.at[j], blocks_out[j], sem.at[j]) for j in range(dp)
    ]
    for copy in copies:
        copy.start()
    for copy in copies:
        copy.wait()


def any_spec():
    return pl.BlockSpec(memory_space=pl.ANY)


def vmem_spec():
    return pl.BlockSpec(memory_space=pltpu.VMEM)


def smem_spec():
    return pl.BlockSpec(memory_space=pltpu.SMEM)


def params_of(flops, moved, limit=38 * MIB):
    return {
        "compiler_params": pltpu.CompilerParams(vmem_limit_bytes=limit),
        "cost_estimate": pl.CostEstimate(
            flops=int(flops), bytes_accessed=int(moved), transcendentals=0
        ),
    }


def shape(dims, dtype):
    return jax.ShapeDtypeStruct(dims, dtype)


def swap(value, axis, flip):
    count = lax.axis_size(axis)
    return lax.ppermute(value, axis, [(i, i ^ flip) for i in range(count)])


def along(value):
    count = lax.axis_size("dp")
    return lax.ppermute(value, "dp", [(i, (i + 2) % count) for i in range(count)])


def pieces_of(value):
    across = swap(value, "seq", 2)
    close = swap(value, "seq", 1)
    return [value, close, across, swap(across, "seq", 1)]


def sum_pieces(value):
    got = swap(value[1], "seq", 1)
    half = (value[0].astype(F32) + got.astype(F32)).astype(BF16)
    other = swap(half[1], "seq", 2)
    return half[0].astype(F32) + other.astype(F32)


def local(inputs, out_grad, segment_ids, params, moment_one, moment_two):
    dp, seq = lax.axis_size("dp"), lax.axis_size("seq")
    length = params.shape[0]
    plan = Plan(dp, seq, length)
    piece = inputs.shape[1]
    tokens = piece * seq
    group, rank = lax.axis_index("dp"), lax.axis_index("seq")
    line = dp // 2
    sublanes = length // LANES
    scratch_rows = up(PAD + sublanes + PAD, 8)
    block = plan.block
    where = plan.scalars(group * seq + rank)
    sc = jnp.stack([rank, group]).astype(jnp.int32)
    place = jnp.asarray(plan.place.reshape(-1))
    row_map = jnp.asarray(plan.row_map)

    flat_params = params.reshape(sublanes, LANES)
    packed = pl.pallas_call(
        functools.partial(pack_kernel, plan),
        out_shape=shape((GROUP, block, LANES), BF16),
        in_specs=[smem_spec(), vmem_spec()],
        out_specs=vmem_spec(),
        scratch_shapes=[
            pltpu.VMEM((scratch_rows, LANES), F32),
            pltpu.VMEM((plan.pure * ROW_SLABS, LANES), F32),
            pltpu.VMEM((plan.frame, LANES), F32),
            pltpu.VMEM((SMALL, LANES), F32),
        ],
        name="pack",
        **params_of(1e6, 2e6),
    )(where, flat_params)
    x_pieces = pieces_of(inputs[0])
    cot = out_grad[0].astype(BF16)
    c_pieces = pieces_of(cot)
    mine = lax.all_to_all(packed, "seq", 0, 0)
    weights = [mine, swap(mine, "dp", 1)]
    ring = mine
    for _ in range(1, line):
        ring = along(ring)
        weights += [ring, swap(ring, "dp", 1)]

    ids = segment_ids[0]
    chunks = tokens // CHUNK
    spot = jnp.arange(tokens)
    by_chunk = ids.reshape(chunks, CHUNK)
    last = by_chunk[:, CHUNK - 1]
    prior = jnp.concatenate([jnp.full((1,), -1, jnp.int32), last[:-1]])
    columns = [ids.astype(F32)]
    for d in range(1, KERNEL):
        earlier = jnp.concatenate([jnp.full((d,), -1, jnp.int32), ids[:-d]])
        columns.append((earlier == ids).astype(F32))
    columns.append((by_chunk == prior[:, None]).reshape(-1).astype(F32))
    columns.append((by_chunk == last[:, None]).reshape(-1).astype(F32))
    columns.append(
        jnp.broadcast_to((last == prior)[:, None], by_chunk.shape).reshape(-1).astype(F32)
    )
    tok = jnp.pad(jnp.stack(columns, axis=1), ((0, 8), (0, LANES - len(columns))))
    segr = by_chunk.astype(F32)

    depth = plan.depth
    limit = 38 * MIB if depth <= 2048 else 63 * MIB
    forward = pl.pallas_call(
        functools.partial(forward_kernel, plan),
        out_shape=[
            shape((tokens, WIDE), BF16),
            shape((tokens, OWN), F32),
            shape((tokens, OWN), F32),
            shape((chunks, STATE, OWN), F32),
            shape((8, tokens), F32),
            shape((depth, WIDE), BF16),
            shape((OWN, D), BF16),
            shape((SMALL, LANES), F32),
            shape((tokens, depth), BF16),
            shape((tokens, D), BF16),
            shape((tokens, D), BF16),
        ],
        in_specs=[smem_spec(), smem_spec(), vmem_spec(), vmem_spec(), vmem_spec()]
        + [any_spec()] * (2 * GROUP + dp),
        out_specs=[vmem_spec()] * 11,
        scratch_shapes=[
            pltpu.VMEM((tokens, D), F32),
            pltpu.VMEM((dp, GROUP, block, LANES), BF16),
            pltpu.VMEM((OUT_SLABS, OWN + plan.frame_rows, LANES), F32),
            pltpu.VMEM((tokens + 8, MIXED), F32),
            pltpu.VMEM((STATE, OWN), F32),
            pltpu.SemaphoreType.DMA((dp + 2 * GROUP,)),
        ],
        name="forward",
        **params_of(8e9, 3e7, limit),
    )(place, sc, row_map, tok, segr, *x_pieces, *c_pieces, *weights)
    proj, ssd, d_gated, states, sums, w_sf, w_out, small, spread, x_hat, cots = forward
    sums = sums + swap(sums, "seq", 1)
    sums = sums + swap(sums, "seq", 2)

    backward = pl.pallas_call(
        functools.partial(backward_kernel, plan),
        out_shape=[shape((GROUP, block, LANES), BF16)] * dp
        + [shape((2, 2, piece, D), BF16)] * 2,
        in_specs=[smem_spec(), smem_spec()] + [vmem_spec()] * 14,
        out_specs=[any_spec()] * dp + [vmem_spec()] * 2,
        scratch_shapes=[
            pltpu.VMEM((dp, GROUP, block, LANES), BF16),
            pltpu.VMEM((tokens + 8, MIXED), F32),
            pltpu.VMEM((tokens + 8, MIXED), F32),
            pltpu.VMEM((STATE, OWN), F32),
            pltpu.VMEM((tokens, OWN), BF16),
            pltpu.VMEM((tokens, WIDE), BF16),
            pltpu.VMEM((CHUNK, LANES), F32),
            pltpu.VMEM((8, OWN), F32),
            pltpu.VMEM((8, OWN), F32),
            pltpu.VMEM((8 * (KERNEL + 1), MIXED), F32),
            pltpu.VMEM((16, LANES), F32),
            pltpu.VMEM((8, D), F32),
            pltpu.VMEM((OUT_SLABS, OWN + plan.frame_rows, LANES), F32),
            pltpu.SemaphoreType.DMA((dp,)),
        ],
        name="backward",
        **params_of(16e9, 4e7, limit),
    )(place, sc, row_map, tok, segr, sums, proj, ssd, d_gated, states, w_sf, w_out, small, spread,
      x_hat, cots)
    terms, act_terms, back_terms = backward[:dp], backward[dp], backward[dp + 1]

    def joined(a, b):
        return (a.astype(F32) + b.astype(F32)).astype(BF16)

    def column(j):
        return joined(terms[2 * j], swap(terms[2 * j + 1], "dp", 1))

    moving = None
    for j in range(line - 1, 0, -1):
        here = column(j)
        moving = along(here if moving is None else joined(here, moving))
    here = column(0)
    reduced = here if moving is None else joined(here, moving)
    blocks = lax.all_to_all(reduced, "seq", 0, 0)

    flat_shape = shape((sublanes, LANES), F32)
    updated = pl.pallas_call(
        functools.partial(unpack_kernel, plan),
        out_shape=[flat_shape] * 4,
        in_specs=[smem_spec()] + [vmem_spec()] * 4,
        out_specs=[vmem_spec()] * 4,
        scratch_shapes=[
            pltpu.VMEM((scratch_rows, LANES), F32),
            pltpu.VMEM((plan.pure * ROW_SLABS, LANES), F32),
            pltpu.VMEM((plan.frame, LANES), F32),
        ],
        name="unpack",
        **params_of(1e6, 5e6),
    )(
        where,
        blocks,
        flat_params,
        moment_one.reshape(sublanes, LANES),
        moment_two.reshape(sublanes, LANES),
    )
    grad, new_params, new_one, new_two = [value.reshape(length) for value in updated]

    residual = inputs[0]
    activation = residual + sum_pieces(act_terms)
    d_normed = sum_pieces(back_terms)
    inv_rms = lax.rsqrt(jnp.mean(residual * residual, axis=-1, keepdims=True) + NORM_EPS)
    hat = residual * inv_rms
    norm_gain = small[25:31].reshape(D)
    d_hat = d_normed * norm_gain
    d_front = inv_rms * (d_hat - hat * jnp.mean(d_hat * hat, axis=-1, keepdims=True))
    gradient = out_grad[0] + d_front
    return (activation[None], gradient[None], grad, new_params, new_one, new_two)


def solution(mesh):
    tokens = P("dp", "seq", None)
    flat = P(("dp", "seq"))

    return jax.shard_map(
        local,
        mesh=mesh,
        in_specs=(tokens, tokens, P("dp", None), flat, flat, flat),
        out_specs=(tokens, tokens, flat, flat, flat, flat),
        check_vma=False,
    )
```

```python
import functools

import jax
import jax.numpy as jnp
import numpy as np
from jax import lax
from jax.experimental import pallas as pl
from jax.experimental.pallas import tpu as pltpu
from jax.sharding import PartitionSpec as P

D = 768
HEADS = 24
HEAD_DIM = 64
STATE = 128
KERNEL = 4
INNER = 1536
PROJ = 3352

NORM_EPS = 1e-05
BETA_ONE = 0.9
BETA_TWO = 0.95
LEARN_RATE = 0.02
WEIGHT_DECAY = 0.1
ADAM_EPS = 1e-08
CORRECT_ONE = 1.0 - BETA_ONE**2
CORRECT_TWO = 1.0 - BETA_TWO**2

LANES = 128
CHUNK = 128
GROUP = 4
OWN = INNER // GROUP
OWN_SLABS = OWN // LANES
MIXED = OWN + 2 * STATE
WIDE = 2 * OWN + 2 * STATE + LANES
SLABS = WIDE // LANES
HEADS_OWN = HEADS // GROUP
IN_SIZE = D * PROJ
OUT_END = IN_SIZE + INNER * D
ROW_SLABS = 32
OUT_SLABS = D // LANES
FRAME = HEAD_DIM * OUT_SLABS
SMALL = 48
PAD = FRAME + 16
MIB = 1024 * 1024

F32 = jnp.float32
BF16 = jnp.bfloat16


def up(value, step):
    return -(-value // step) * step


class Plan:
    def __init__(self, dp, seq, length):
        self.dp, self.seq, self.length = dp, seq, length
        count = dp * seq
        self.count = count
        self.first_out = IN_SIZE // length
        assert seq == GROUP and dp % 2 == 0 and length % LANES == 0
        assert IN_SIZE % length and (count - 1) * length <= OUT_END
        start = [i * length for i in range(count)]
        rows = []
        for i in range(self.first_out + 1):
            first = start[i] // PROJ
            last = (min(start[i] + length, IN_SIZE) - 1) // PROJ
            rows.append((first, last - first + 1))
        self.rows = rows
        self.pure = up(max(n for _, n in rows[:-1]), 16)
        self.edge = up(rows[-1][1], 16)
        self.most_rows = max(n for _, n in rows)
        edge_out = -(-(start[self.first_out] + length - IN_SIZE) // D)
        assert edge_out <= HEAD_DIM
        self.edge_out = up(edge_out, 8)
        self.edge_at = SLABS * self.edge
        self.small_row = (OUT_END - start[-1]) // LANES
        place = np.zeros((count, GROUP), np.int32)
        for i in range(self.first_out, count):
            low = max(start[i] - IN_SIZE, 0) // D // HEAD_DIM
            high = (min(start[i] + length, OUT_END) - 1 - IN_SIZE) // D // HEAD_DIM
            assert high - low < GROUP
            for head in range(low, high + 1):
                place[i, head % GROUP] = head // GROUP
        self.place = place
        self.frame_rows = HEAD_DIM if length > D * HEAD_DIM else up(length // D + 2, 8)
        if self.frame_rows < HEAD_DIM:
            for i in range(self.first_out, count):
                for rank in range(GROUP):
                    begin = max(start[i] - IN_SIZE, 0) // D
                    head = self.place[i, rank] * GROUP + rank
                    self.place[i, rank] = self.place[i, rank] * HEAD_DIM + max(
                        begin - head * HEAD_DIM, 0
                    )
        else:
            self.place = self.place * HEAD_DIM
        self.frame = self.frame_rows * OUT_SLABS
        need = max(
            SLABS * self.pure, self.edge_at + OUT_SLABS * self.edge_out, self.frame + SMALL
        )
        self.block = up(need, 16)

    def scalars(self, index):
        begin = index * self.length
        first = begin // PROJ
        last = (jnp.minimum(begin + self.length, IN_SIZE) - 1) // PROJ
        form = jnp.where(index < self.first_out, 0, jnp.where(index == self.first_out, 1, 2))
        low = jnp.maximum(begin - IN_SIZE, 0) // D // HEAD_DIM
        high = (jnp.minimum(begin + self.length, OUT_END) - 1 - IN_SIZE) // D // HEAD_DIM
        values = [form, first * PROJ - begin, last - first + 1, index == self.count - 1]
        counts = []
        for rank in range(GROUP):
            head = low + (rank - low) % GROUP
            row = head * HEAD_DIM
            rows = HEAD_DIM
            if self.frame_rows < HEAD_DIM:
                top = jnp.maximum(begin - IN_SIZE, 0) // D
                bottom = (jnp.minimum(begin + self.length, OUT_END) - 1 - IN_SIZE) // D + 1
                rows = jnp.minimum(row + HEAD_DIM, bottom) - jnp.maximum(row, top)
                row = jnp.maximum(row, top)
            at = (IN_SIZE + row * D - begin) // LANES
            held = (head <= high) & (form > 0)
            values.append(jnp.where(held, at, -PAD))
            counts.append(jnp.where(held, rows * OUT_SLABS, 0))
        values += counts + [index % GROUP]
        return jnp.stack([jnp.asarray(v, jnp.int32) for v in values])


def lane_iota(rows):
    return lax.broadcasted_iota(jnp.int32, (rows, LANES), 1)


def join_halves(first, second, rank):
    lane = lane_iota(first.shape[0])
    if rank % 2 == 0:
        return jnp.where(lane < 64, first, pltpu.roll(second, 64, 1))
    return jnp.where(lane < 64, pltpu.roll(first, 64, 1), second)


def own_slab(get, rank, slab):
    return join_halves(get(4 * slab + rank // 2), get(4 * slab + 2 + rank // 2), rank)


def whole_slab(get, slab):
    half = (slab // 2) % 2
    return join_halves(get((2 * slab) % 4, slab // 4), get((2 * slab + 1) % 4, slab // 4), half)


def pack_kernel(plan, sc, x_ref, out_ref, flat, rowbuf, frame, small):
    local = x_ref.shape[0]
    flat[...] = jnp.zeros_like(flat)
    flat[PAD : PAD + local, :] = x_ref[...]
    out_ref[...] = jnp.zeros_like(out_ref)
    lane = lane_iota(ROW_SLABS)
    form = sc[0]

    @pl.when(form < 2)
    def _():
        rowbuf[...] = jnp.zeros_like(rowbuf)

        def row(r, carry):
            at = sc[1] + r * PROJ + PAD * LANES
            sub, shift = at // LANES, at % LANES
            turn = (LANES - shift) % LANES
            near = pltpu.roll(flat[pl.ds(sub, ROW_SLABS), :], turn, 1)
            far = pltpu.roll(flat[pl.ds(sub + 1, ROW_SLABS), :], turn, 1)
            joined = jnp.where(lane < LANES - shift, near, far)
            rowbuf[pl.ds(pl.multiple_of(r * ROW_SLABS, ROW_SLABS), ROW_SLABS), :] = jnp.where(
                r < sc[2], joined, 0.0
            )
            return carry

        lax.fori_loop(0, plan.most_rows, row, 0)

    def weights(depth):
        def get(column):
            return rowbuf[pl.ds(column, depth, stride=ROW_SLABS), :]

        def put(rank, j, slab):
            out_ref[rank ^ sc[12], j * depth : (j + 1) * depth, :] = slab.astype(BF16)

        for half in range(2):
            for m in range(OWN_SLABS):
                cols = [get(12 * half + 4 * m + c) for c in range(4)]
                for rank in range(GROUP):
                    slab = join_halves(cols[rank // 2], cols[2 + rank // 2], rank)
                    put(rank, OWN_SLABS * half + m, slab)
        rest = [get(24), get(25), jnp.where(lane_iota(depth) < HEADS, get(26), 0.0)]
        for rank in range(GROUP):
            for j, slab in enumerate(rest):
                put(rank, 2 * OWN_SLABS + j, slab)

    @pl.when(form == 0)
    def _():
        weights(plan.pure)

    @pl.when(form == 1)
    def _():
        weights(plan.edge)

    def frames(rows, base):
        for rank in range(GROUP):
            row = lax.broadcasted_iota(jnp.int32, (plan.frame, LANES), 0)
            frame[...] = jnp.where(
                row < sc[8 + rank], flat[pl.ds(sc[4 + rank] + PAD, plan.frame), :], 0.0
            )
            for j in range(OUT_SLABS):
                out_ref[rank ^ sc[12], base + j * rows : base + (j + 1) * rows, :] = frame[
                    pl.ds(j, rows, stride=OUT_SLABS), :
                ].astype(BF16)

    @pl.when(form == 1)
    def _():
        frames(plan.edge_out, plan.edge_at)

    @pl.when(form == 2)
    def _():
        frames(plan.frame_rows, 0)

    @pl.when(sc[3] == 1)
    def _():
        base = PAD + plan.small_row

        def get(row):
            return flat[base + row : base + row + 1, :]

        small[...] = jnp.zeros_like(small)
        for rank in range(GROUP):
            at = 0
            for k in range(KERNEL + 1):
                for m in range(OWN_SLABS):
                    small[at : at + 1, :] = own_slab(lambda c: get(14 * k + c), rank, m)
                    at += 1
                for row in (12, 13):
                    small[at : at + 1, :] = get(14 * k + row)
                    at += 1
            for row in range(70, 76):
                small[at : at + 1, :] = get(row)
                at += 1
            for m in range(OWN_SLABS):
                small[at : at + 1, :] = own_slab(lambda c: get(76 + c), rank, m)
                at += 1
            small[at : at + 1, :] = get(88)
            out_ref[rank ^ sc[12], plan.frame : plan.frame + SMALL, :] = small[...].astype(BF16)


def unpack_kernel(
    plan, sc, blk, par, one, two, grad_ref, par_ref, one_ref, two_ref, flat, rowbuf, frame
):
    local = par.shape[0]
    flat[...] = jnp.zeros_like(flat)
    lane = lane_iota(ROW_SLABS)
    form = sc[0]

    def total(at, rows):
        parts = [blk[rank ^ sc[12], at : at + rows, :].astype(F32) for rank in range(GROUP)]
        return (parts[0] + parts[1]) + (parts[2] + parts[3])

    def weights(depth):
        rowbuf[...] = jnp.zeros_like(rowbuf)

        def get(base):
            def piece(rank, m):
                at = (base + m) * depth
                return blk[rank ^ sc[12], at : at + depth, :].astype(F32)

            return piece

        for half in range(2):
            for j in range(12):
                rowbuf[pl.ds(12 * half + j, depth, stride=ROW_SLABS), :] = whole_slab(
                    get(OWN_SLABS * half), j
                )
        for j in range(3):
            rowbuf[pl.ds(24 + j, depth, stride=ROW_SLABS), :] = total((6 + j) * depth, depth)

    def rows():
        def row(r, carry):
            at = sc[1] + r * PROJ + PAD * LANES
            sub, shift = at // LANES, at % LANES
            value = rowbuf[pl.ds(pl.multiple_of(r * ROW_SLABS, ROW_SLABS), ROW_SLABS), :]
            value = pltpu.roll(jnp.where(r < sc[2], value, 0.0), shift, 1)
            flat[pl.ds(sub, ROW_SLABS), :] += jnp.where(lane >= shift, value, 0.0)
            flat[pl.ds(sub + 1, ROW_SLABS), :] += jnp.where(lane < shift, value, 0.0)
            return carry

        lax.fori_loop(0, plan.most_rows, row, 0)

    def frames(count, base):
        for rank in range(GROUP):
            frame[...] = jnp.zeros_like(frame)
            for j in range(OUT_SLABS):
                frame[pl.ds(j, count, stride=OUT_SLABS), :] = blk[
                    rank ^ sc[12], base + j * count : base + (j + 1) * count, :
                ].astype(F32)
            row = lax.broadcasted_iota(jnp.int32, (plan.frame, LANES), 0)
            flat[pl.ds(sc[4 + rank] + PAD, plan.frame), :] += jnp.where(
                row < sc[8 + rank], frame[...], 0.0
            )

    @pl.when(form == 0)
    def _():
        weights(plan.pure)
        rows()

    @pl.when(form == 1)
    def _():
        frames(plan.edge_out, plan.edge_at)
        weights(plan.edge)
        rows()

    @pl.when(form == 2)
    def _():
        frames(plan.frame_rows, 0)

    @pl.when(sc[3] == 1)
    def _():
        base = PAD + plan.small_row
        rows = [blk[rank ^ sc[12], plan.frame : plan.frame + SMALL, :].astype(F32) for rank in range(GROUP)]
        summed = (rows[0] + rows[1]) + (rows[2] + rows[3])

        def get(start):
            return lambda rank, m: rows[rank][start + m : start + m + 1]

        for k in range(KERNEL + 1):
            at = base + 14 * k
            for j in range(12):
                flat[at + j : at + j + 1, :] = whole_slab(get(5 * k), j)
            flat[at + 12 : at + 14, :] = summed[5 * k + 3 : 5 * k + 5]
        flat[base + 70 : base + 76, :] = summed[25:31]
        for j in range(12):
            flat[base + 76 + j : base + 77 + j, :] = whole_slab(get(31), j)
        flat[base + 88 : base + 89, :] = summed[34:35]

    grad = flat[PAD : PAD + local, :]
    new_one = BETA_ONE * one[...] + (1.0 - BETA_ONE) * grad
    new_two = BETA_TWO * two[...] + (1.0 - BETA_TWO) * grad * grad
    params = par[...]
    grad_ref[...] = grad
    one_ref[...] = new_one
    two_ref[...] = new_two
    par_ref[...] = params - LEARN_RATE * (
        new_one / CORRECT_ONE / (jnp.sqrt(new_two / CORRECT_TWO) + ADAM_EPS)
        + WEIGHT_DECAY * params
    )


def mm(a, b):
    return lax.dot_general(a, b, (((1,), (0,)), ((), ())), preferred_element_type=F32)


def mm_nt(a, b):
    return lax.dot_general(a, b, (((1,), (1,)), ((), ())), preferred_element_type=F32)


def mm_tn(a, b):
    return lax.dot_general(a, b, (((0,), (0,)), ((), ())), preferred_element_type=F32)


def thirds(value):
    high = value.astype(BF16)
    rest = value - high.astype(F32)
    middle = rest.astype(BF16)
    return high, middle, (rest - middle.astype(F32)).astype(BF16)


def expand(value):
    rows = value.shape[0]
    lane = lane_iota(rows)
    return jnp.concatenate(
        [
            jnp.where(lane < 64, value[:, 8 * m : 8 * m + 1], value[:, 8 * m + 4 : 8 * m + 5])
            for m in range(OWN_SLABS)
        ],
        axis=1,
    )


def head_sums(value):
    row = lax.broadcasted_iota(jnp.int32, (OWN, LANES), 0)
    col = lax.broadcasted_iota(jnp.int32, (OWN, LANES), 1)
    pick = (col == GROUP * (row // HEAD_DIM)).astype(BF16)
    high = value.astype(BF16)
    low = (value - high.astype(F32)).astype(BF16)
    return mm(high, pick) + mm(low, pick)


def small_rows(small, start, count):
    return jnp.concatenate([small[start + m : start + m + 1, :] for m in range(count)], axis=1)


class Small:
    def __init__(self, small, rank):
        self.taps = [small_rows(small, 5 * k, 5) for k in range(KERNEL)]
        self.conv_bias = small_rows(small, 20, 5)
        self.gated_gain = small_rows(small, 31, OWN_SLABS)
        vec = small[34:35, :]
        lane = lane_iota(1)
        self.heads = (lane % GROUP == 0) & (lane < HEADS)

        def pick(at):
            turned = pltpu.roll(vec, (2 * LANES - at - rank) % LANES, 1)
            return jnp.where(self.heads, turned, 0.0)

        self.delta_bias = pick(0)
        self.rate = jnp.where(self.heads, -jnp.exp(pick(HEADS)), 0.0)
        self.skip = expand(pick(2 * HEADS))


def triangle(lower):
    row = lax.broadcasted_iota(jnp.int32, (CHUNK, CHUNK), 0)
    col = lax.broadcasted_iota(jnp.int32, (CHUNK, CHUNK), 1)
    return (row >= col) if lower else (row <= col)


class Front:
    def __init__(self, c, rank, sm, xf, proj, tok, segr):
        at = pl.multiple_of(c * CHUNK, CHUNK)
        window = xf[pl.ds(at, CHUNK + 8), :]
        self.shifted = [window[8 - d : 8 - d + CHUNK] for d in range(KERNEL)]
        tk = tok[pl.ds(at, CHUNK), :]
        self.masks = [None] + [tk[:, d : d + 1] for d in range(1, KERNEL)]
        conv = sm.conv_bias + sm.taps[KERNEL - 1] * self.shifted[0]
        for d in range(1, KERNEL):
            conv = conv + sm.taps[KERNEL - 1 - d] * self.shifted[d] * self.masks[d]
        self.conv = conv
        self.conv_sig = jax.nn.sigmoid(conv)
        act = conv * self.conv_sig
        self.values = act[:, :OWN]
        self.b = act[:, OWN : OWN + STATE].astype(BF16)
        self.c = act[:, OWN + STATE :].astype(BF16)
        raw = proj[pl.ds(at, CHUNK), WIDE - LANES :].astype(F32)
        pre = pltpu.roll(raw, (LANES - rank) % LANES, 1) + sm.delta_bias
        self.pre = pre
        self.step = jnp.where(
            sm.heads, jnp.maximum(pre, 0.0) + jnp.log1p(jnp.exp(-jnp.abs(pre))), 0.0
        )
        log_decay = self.step * sm.rate
        lower = triangle(True)
        ones = lower.astype(BF16)
        high, middle, low = thirds(log_decay)
        sums = mm(ones, high) + (mm(ones, middle) + mm(ones, low))
        self.sums = sums
        self.sums_t = sums.T
        last = sums[CHUNK - 1 : CHUNK, :]
        self.allowed = (tk[:, 0:1] == segr[pl.ds(c, 1), :]) & lower
        self.step_wide = expand(self.step)
        self.scaled = self.values * self.step_wide
        self.scaled_n = self.scaled.astype(BF16)
        self.head_in = expand(jnp.exp(sums) * tk[:, 4:5])
        self.tail = expand(jnp.exp(last - sums) * tk[:, 5:6])
        self.carry = expand(jnp.exp(last) * tk[CHUNK - 1 : CHUNK, 6:7])
        self.tail_scaled = self.tail * self.scaled
        self.scores = mm_nt(self.c, self.b)
        gate = proj[pl.ds(at, CHUNK), :OWN].astype(F32)
        self.gate = gate
        self.gate_sig = jax.nn.sigmoid(gate)
        self.gate_act = gate * self.gate_sig

    def decay(self, k):
        gap = self.sums[:, 4 * k : 4 * k + 1] - self.sums_t[4 * k : 4 * k + 1, :]
        return jnp.exp(jnp.where(self.allowed, gap, -1e30))

    def head(self, value, k):
        return value[:, HEAD_DIM * k : HEAD_DIM * (k + 1)]


def fill_xf(xf, proj, tokens):
    xf[0:8, :] = jnp.zeros((8, MIXED), F32)
    xf[8 : 8 + tokens, :] = proj[:, OWN : OWN + MIXED].astype(F32)


def forward_kernel(plan, place, sc, tok, segr, *refs):
    dp = plan.dp
    x_in, c_in, w_in = refs[:4], refs[4:8], refs[8 : 8 + dp]
    refs = refs[8 + dp :]
    (proj, ssd, d_gated, states, sums_ref, w_in_ref, w_out, small_ref, normed, x_hat, cots) = refs[:11]
    xs, blocks, w_rows, w_acc, xf, state, sem = refs[11:]
    tokens = xs.shape[0]
    piece = tokens // GROUP
    rank, group = sc[0], sc[1]
    line = dp // 2
    copies = []
    for j in range(dp):
        where = lax.rem(group // 2 + line - j // 2, line) * 2 + lax.rem(group + j % 2, 2)
        copies.append(pltpu.make_async_copy(w_in[j], blocks.at[where], sem.at[j]))
    for r in range(GROUP):
        at = pl.multiple_of((rank ^ r) * piece, piece)
        copies.append(pltpu.make_async_copy(x_in[r], xs.at[pl.ds(at, piece)], sem.at[dp + r]))
        copies.append(
            pltpu.make_async_copy(c_in[r], cots.at[pl.ds(at, piece)], sem.at[dp + GROUP + r])
        )
    for copy in copies:
        copy.start()
    for copy in copies:
        copy.wait()
    w_rows[...] = jnp.zeros_like(w_rows)

    def rows_of(i, at, depth):
        for j in range(SLABS):
            w_rows[j, pl.ds(at, depth), :] += blocks[
                i // GROUP, (i % GROUP) ^ rank, j * depth : (j + 1) * depth, :
            ].astype(F32)

    def pure_rows(i, carry):
        rows_of(i, (i * plan.length) // PROJ, plan.pure)
        return carry

    lax.fori_loop(0, plan.first_out, pure_rows, 0)
    rows_of(plan.first_out, plan.rows[-1][0], plan.edge)
    for j in range(SLABS):
        w_in_ref[:, j * LANES : (j + 1) * LANES] = w_rows[j, 0:D, :].astype(BF16)
    w_acc[...] = jnp.zeros_like(w_acc)
    for i in range(plan.first_out, plan.count):
        rows, base = (plan.edge_out, plan.edge_at) if i == plan.first_out else (plan.frame_rows, 0)
        at = place[i * GROUP + rank]
        if plan.frame_rows == HEAD_DIM:
            at = pl.multiple_of(at, HEAD_DIM)
        for j in range(OUT_SLABS):
            w_acc[j, pl.ds(at, rows), :] += blocks[
                i // GROUP, (i % GROUP) ^ rank, base + j * rows : base + (j + 1) * rows, :
            ].astype(F32)
    for j in range(OUT_SLABS):
        w_out[:, j * LANES : (j + 1) * LANES] = w_acc[j, 0:OWN, :].astype(BF16)
    small = blocks[dp - 1, (GROUP - 1) ^ rank, plan.frame : plan.frame + SMALL, :].astype(F32)
    small_ref[...] = small
    sm = Small(small, rank)
    norm_gain = small_rows(small, 25, OUT_SLABS)

    def tile(t, carry):
        at = pl.ds(pl.multiple_of(t * 256, 256), 256)
        x = xs[at, :]
        scale = lax.rsqrt(jnp.sum(x * x, axis=1, keepdims=True) * (1.0 / D) + NORM_EPS)
        unit = x * scale
        x_hat[at, :] = unit.astype(BF16)
        scaled = (unit * norm_gain).astype(BF16)
        normed[at, :] = scaled
        proj[at, :] = mm(scaled, w_in_ref[...]).astype(BF16)
        d_gated[at, :] = mm_nt(cots[at, :], w_out[...])
        return carry

    lax.fori_loop(0, tokens // 256, tile, 0)
    fill_xf(xf, proj, tokens)
    state[...] = jnp.zeros_like(state)

    def chunk(c, carry):
        at = pl.ds(pl.multiple_of(c * CHUNK, CHUNK), CHUNK)
        f = Front(c, rank, sm, xf, proj, tok, segr)
        inner = []
        for k in range(HEADS_OWN):
            weighted = (f.decay(k) * f.scores).astype(BF16)
            inner.append(mm(weighted, f.head(f.scaled_n, k)))
        entering = state[...]
        states[c] = entering
        through = mm(f.c, entering.astype(BF16))
        out = jnp.concatenate(inner, axis=1) + through * f.head_in + sm.skip * f.values
        ssd[at, :] = out
        state[...] = f.carry * entering + mm_tn(f.b, f.tail_scaled.astype(BF16))
        mixed = out * f.gate_act
        first = jnp.sum(mixed * mixed, axis=1, keepdims=True)
        second = jnp.sum(d_gated[at, :] * sm.gated_gain * mixed, axis=1, keepdims=True)
        both = jnp.where(lane_iota(CHUNK) == 0, first, second)
        sums_ref[:, at] = both.T[0:8, :]
        return carry

    lax.fori_loop(0, tokens // CHUNK, chunk, 0)


def fold(value):
    rows, width = value.shape
    return jnp.sum(value.reshape(rows // 8, 8, width), axis=0)


def backward_kernel(
    plan, place, sc, tok, segr, sums_ref, proj, ssd, d_gated, states, w_in, w_out, small_ref, normed, x_hat, cots, *refs
):
    dp = plan.dp
    blocks_out, act_out, back_out = refs[:dp], refs[dp], refs[dp + 1]
    (blocks, xf, dcf, adjoint, gated, dn, colbuf, acc_gg, acc_skip, acc_conv, acc_head, acc_ng,
     wide_in, wide_out, sem) = refs[dp + 2 :]
    tokens = proj.shape[0]
    piece = tokens // GROUP
    rank, group = sc[0], sc[1]
    chunks = tokens // CHUNK
    sm = Small(small_ref[...], rank)
    fill_xf(xf, proj, tokens)
    for ref in (dcf, adjoint, colbuf, acc_gg, acc_skip, acc_conv, acc_head, acc_ng):
        ref[...] = jnp.zeros_like(ref)
    lane = lane_iota(CHUNK)

    def chunk(i, carry):
        c = chunks - 1 - i
        start = pl.multiple_of(c * CHUNK, CHUNK)
        at = pl.ds(start, CHUNK)
        f = Front(c, rank, sm, xf, proj, tok, segr)
        both = jnp.concatenate([sums_ref[:, at]] * (CHUNK // 8), axis=0).T
        norm = lax.rsqrt(both[:, 0:1] * (1.0 / INNER) + NORM_EPS)
        drag = norm * (both[:, 1:2] * (1.0 / INNER))
        out = ssd[at, :]
        dg = d_gated[at, :]
        unit = out * f.gate_act * norm
        gated[at, :] = (unit * sm.gated_gain).astype(BF16)
        acc_gg[...] += fold(dg * unit)
        d_mixed = norm * (dg * sm.gated_gain - unit * drag)
        d_ssd = d_mixed * f.gate_act
        d_gate = d_mixed * out * (f.gate_sig * (1.0 + f.gate * (1.0 - f.gate_sig)))
        acc_skip[...] += fold(d_ssd * f.values)
        d_ssd_n = d_ssd.astype(BF16)
        entering = states[c]
        entering_n = entering.astype(BF16)
        leaving = adjoint[...]
        leaving_n = leaving.astype(BF16)
        head_ssd = f.head_in * d_ssd
        head_ssd_n = head_ssd.astype(BF16)
        through = mm(f.c, entering_n)
        exit_b = mm(f.b, leaving_n)
        tail_flow = f.tail_scaled * exit_b
        last_row = jnp.sum(tail_flow, axis=0, keepdims=True) + f.carry * jnp.sum(
            leaving * entering, axis=0, keepdims=True
        )
        row = lax.broadcasted_iota(jnp.int32, (CHUNK, OWN), 0)
        flow = head_ssd * through - tail_flow + jnp.where(row == CHUNK - 1, last_row, 0.0)
        d_scores = jnp.zeros((CHUNK, CHUNK), F32)
        d_scaled = []
        row_sums = jnp.zeros((CHUNK, LANES), F32)
        for k in range(HEADS_OWN):
            decay = f.decay(k)
            weighted = decay * f.scores
            d_head = f.head(d_ssd_n, k)
            d_weighted = mm_nt(d_head, f.head(f.scaled_n, k))
            d_scaled.append(mm_tn(weighted.astype(BF16), d_head))
            d_scores = d_scores + d_weighted * decay
            flows = d_weighted * weighted
            row_sums = jnp.where(lane == 4 * k, jnp.sum(flows, axis=1, keepdims=True), row_sums)
            colbuf[4 * k : 4 * k + 1, :] = jnp.sum(flows, axis=0, keepdims=True)
        d_scaled = jnp.concatenate(d_scaled, axis=1) + f.tail * exit_b
        d_scores_n = d_scores.astype(BF16)
        d_c = mm_nt(head_ssd_n, entering_n) + mm(d_scores_n, f.b)
        d_b = mm_tn(d_scores_n, f.c) + mm_nt(f.tail_scaled.astype(BF16), leaving_n)
        adjoint[...] = f.carry * leaving + mm_tn(f.c, head_ssd_n)
        d_sums = row_sums - colbuf[...].T + head_sums(flow)
        upper = triangle(False).astype(BF16)
        high, middle, low = thirds(d_sums)
        d_log = mm(upper, high) + (mm(upper, middle) + mm(upper, low))
        d_values = sm.skip * d_ssd + d_scaled * f.step_wide
        d_step = head_sums(d_scaled * f.values) + d_log * sm.rate
        d_raw = jnp.where(sm.heads, d_step * jax.nn.sigmoid(f.pre), 0.0)
        acc_head[0:8, :] += fold(d_raw)
        acc_head[8:16, :] += fold(d_log * f.step) * sm.rate
        d_act = jnp.concatenate([d_values, d_b, d_c], axis=1)
        d_conv = d_act * (f.conv_sig * (1.0 + f.conv * (1.0 - f.conv_sig)))
        acc_conv[8 * KERNEL : 8 * KERNEL + 8, :] += fold(d_conv)
        acc_conv[8 * (KERNEL - 1) : 8 * KERNEL, :] += fold(d_conv * f.shifted[0])
        for d in range(1, KERNEL):
            lower = 8 * (KERNEL - 1 - d)
            acc_conv[lower : lower + 8, :] += fold(d_conv * f.shifted[d] * f.masks[d])
        dcf[at, :] = d_conv
        window = dcf[pl.ds(start, CHUNK + 8), :]
        masks = tok[pl.ds(start, CHUNK + 8), :]
        d_x = sm.taps[KERNEL - 1] * d_conv
        for d in range(1, KERNEL):
            masked = window * masks[:, d : d + 1]
            d_x = d_x + sm.taps[KERNEL - 1 - d] * masked[d : d + CHUNK]
        dn[at, 0:OWN] = d_gate.astype(BF16)
        dn[at, OWN : OWN + MIXED] = d_x.astype(BF16)
        dn[at, WIDE - LANES :] = pltpu.roll(d_raw, rank, 1).astype(BF16)
        return carry

    lax.fori_loop(0, chunks, chunk, 0)

    for token_group in range(GROUP):
        rel = token_group ^ rank
        at = slice(token_group * piece, (token_group + 1) * piece)
        act_out[lax.rem(rel, 2), rel // 2] = mm(gated[at, :], w_out[...]).astype(BF16)
        d_normed = mm_nt(dn[at, :], w_in[...])
        back_out[lax.rem(rel, 2), rel // 2] = d_normed.astype(BF16)
        acc_ng[...] += fold(d_normed * x_hat[at, :].astype(F32))

    line = dp // 2

    def slot(i):
        to = i // GROUP
        return lax.rem(to // 2 + line - group // 2, line) * 2 + (lax.rem(to + group, 2))

    grad_in = mm_tn(normed[...], dn[...])
    for j in range(SLABS):
        wide_in[j, 0:D, :] = grad_in[:, j * LANES : (j + 1) * LANES]
        wide_in[j, D:, :] = jnp.zeros((plan.pure, LANES), F32)

    def rows_of(i, at, depth):
        to = slot(i)
        for j in range(SLABS):
            blocks[to, (i % GROUP) ^ rank, j * depth : (j + 1) * depth, :] = wide_in[
                j, pl.ds(at, depth), :
            ].astype(BF16)

    def pure_rows(i, carry):
        rows_of(i, (i * plan.length) // PROJ, plan.pure)
        return carry

    lax.fori_loop(0, plan.first_out, pure_rows, 0)
    rows_of(plan.first_out, plan.rows[-1][0], plan.edge)
    grad_out = mm_tn(gated[...], cots[...])
    for j in range(OUT_SLABS):
        wide_out[j, 0:OWN, :] = grad_out[:, j * LANES : (j + 1) * LANES]
        wide_out[j, OWN:, :] = jnp.zeros((plan.frame_rows, LANES), F32)
    for i in range(plan.first_out, plan.count):
        rows, base = (plan.edge_out, plan.edge_at) if i == plan.first_out else (plan.frame_rows, 0)
        at = place[i * GROUP + rank]
        if plan.frame_rows == HEAD_DIM:
            at = pl.multiple_of(at, HEAD_DIM)
        to = slot(i)
        for j in range(OUT_SLABS):
            blocks[to, (i % GROUP) ^ rank, base + j * rows : base + (j + 1) * rows, :] = wide_out[
                j, pl.ds(at, rows), :
            ].astype(BF16)
    tail = []
    for k in range(KERNEL + 1):
        line_sum = jnp.sum(acc_conv[8 * k : 8 * k + 8, :], axis=0, keepdims=True)
        tail += [line_sum[:, m * LANES : (m + 1) * LANES] for m in range(5)]
    gain = jnp.sum(acc_ng[...], axis=0, keepdims=True)
    tail += [gain[:, m * LANES : (m + 1) * LANES] for m in range(OUT_SLABS)]
    gain = jnp.sum(acc_gg[...], axis=0, keepdims=True)
    tail += [gain[:, m * LANES : (m + 1) * LANES] for m in range(OWN_SLABS)]
    bias = jnp.sum(acc_head[0:8, :], axis=0, keepdims=True)
    rate = jnp.sum(acc_head[8:16, :], axis=0, keepdims=True)
    skip = jnp.sum(head_sums(acc_skip[...]), axis=0, keepdims=True)
    heads = sm.heads
    vec = pltpu.roll(jnp.where(heads, bias, 0.0), rank, 1)
    vec = vec + pltpu.roll(jnp.where(heads, rate, 0.0), rank + HEADS, 1)
    vec = vec + pltpu.roll(jnp.where(heads, skip, 0.0), rank + 2 * HEADS, 1)
    tail += [vec, jnp.zeros((SMALL - len(tail) - 1, LANES), F32)]
    blocks[slot(plan.count - 1), (GROUP - 1) ^ rank, plan.frame : plan.frame + SMALL, :] = jnp.concatenate(
        tail, axis=0
    ).astype(BF16)
    copies = [
        pltpu.make_async_copy(blocks.at[j], blocks_out[j], sem.at[j]) for j in range(dp)
    ]
    for copy in copies:
        copy.start()
    for copy in copies:
        copy.wait()


def any_spec():
    return pl.BlockSpec(memory_space=pl.ANY)


def vmem_spec():
    return pl.BlockSpec(memory_space=pltpu.VMEM)


def smem_spec():
    return pl.BlockSpec(memory_space=pltpu.SMEM)


def params_of(flops, moved, limit=38 * MIB):
    return {
        "compiler_params": pltpu.CompilerParams(vmem_limit_bytes=limit),
        "cost_estimate": pl.CostEstimate(
            flops=int(flops), bytes_accessed=int(moved), transcendentals=0
        ),
    }


def shape(dims, dtype):
    return jax.ShapeDtypeStruct(dims, dtype)


def swap(value, axis, flip):
    count = lax.axis_size(axis)
    return lax.ppermute(value, axis, [(i, i ^ flip) for i in range(count)])


def along(value):
    count = lax.axis_size("dp")
    return lax.ppermute(value, "dp", [(i, (i + 2) % count) for i in range(count)])


def pieces_of(value):
    across = swap(value, "seq", 2)
    close = swap(value, "seq", 1)
    return [value, close, across, swap(across, "seq", 1)]


def exchange(value):
    return jnp.stack([value[0]] + [swap(value[r], "seq", r) for r in range(1, GROUP)])


def sum_pieces(value):
    got = swap(value[1], "seq", 1)
    half = (value[0].astype(F32) + got.astype(F32)).astype(BF16)
    other = swap(half[1], "seq", 2)
    return half[0].astype(F32) + other.astype(F32)


def local(inputs, out_grad, segment_ids, params, moment_one, moment_two):
    dp, seq = lax.axis_size("dp"), lax.axis_size("seq")
    length = params.shape[0]
    plan = Plan(dp, seq, length)
    piece = inputs.shape[1]
    tokens = piece * seq
    group, rank = lax.axis_index("dp"), lax.axis_index("seq")
    line = dp // 2
    sublanes = length // LANES
    scratch_rows = up(PAD + sublanes + PAD, 8)
    block = plan.block
    where = plan.scalars(group * seq + rank)
    sc = jnp.stack([rank, group]).astype(jnp.int32)
    place = jnp.asarray(plan.place.reshape(-1))

    flat_params = params.reshape(sublanes, LANES)
    packed = pl.pallas_call(
        functools.partial(pack_kernel, plan),
        out_shape=shape((GROUP, block, LANES), BF16),
        in_specs=[smem_spec(), vmem_spec()],
        out_specs=vmem_spec(),
        scratch_shapes=[
            pltpu.VMEM((scratch_rows, LANES), F32),
            pltpu.VMEM((plan.pure * ROW_SLABS, LANES), F32),
            pltpu.VMEM((plan.frame, LANES), F32),
            pltpu.VMEM((SMALL, LANES), F32),
        ],
        name="pack",
        **params_of(1e6, 2e6),
    )(where, flat_params)
    x_pieces = pieces_of(inputs[0])
    cot = out_grad[0].astype(BF16)
    c_pieces = pieces_of(cot)
    mine = exchange(packed)
    weights = [mine, swap(mine, "dp", 1)]
    ring = mine
    for _ in range(1, line):
        ring = along(ring)
        weights += [ring, swap(ring, "dp", 1)]

    ids = segment_ids[0]
    chunks = tokens // CHUNK
    spot = jnp.arange(tokens)
    by_chunk = ids.reshape(chunks, CHUNK)
    last = by_chunk[:, CHUNK - 1]
    prior = jnp.concatenate([jnp.full((1,), -1, jnp.int32), last[:-1]])
    columns = [ids.astype(F32)]
    for d in range(1, KERNEL):
        earlier = jnp.concatenate([jnp.full((d,), -1, jnp.int32), ids[:-d]])
        columns.append((earlier == ids).astype(F32))
    columns.append((by_chunk == prior[:, None]).reshape(-1).astype(F32))
    columns.append((by_chunk == last[:, None]).reshape(-1).astype(F32))
    columns.append(
        jnp.broadcast_to((last == prior)[:, None], by_chunk.shape).reshape(-1).astype(F32)
    )
    tok = jnp.pad(jnp.stack(columns, axis=1), ((0, 8), (0, LANES - len(columns))))
    segr = by_chunk.astype(F32)

    limit = 38 * MIB if dp <= 8 else 63 * MIB
    forward = pl.pallas_call(
        functools.partial(forward_kernel, plan),
        out_shape=[
            shape((tokens, WIDE), BF16),
            shape((tokens, OWN), F32),
            shape((tokens, OWN), F32),
            shape((chunks, STATE, OWN), F32),
            shape((8, tokens), F32),
            shape((D, WIDE), BF16),
            shape((OWN, D), BF16),
            shape((SMALL, LANES), F32),
            shape((tokens, D), BF16),
            shape((tokens, D), BF16),
            shape((tokens, D), BF16),
        ],
        in_specs=[smem_spec(), smem_spec(), vmem_spec(), vmem_spec()]
        + [any_spec()] * (2 * GROUP + dp),
        out_specs=[vmem_spec()] * 11,
        scratch_shapes=[
            pltpu.VMEM((tokens, D), F32),
            pltpu.VMEM((dp, GROUP, block, LANES), BF16),
            pltpu.VMEM((SLABS, D + plan.pure, LANES), F32),
            pltpu.VMEM((OUT_SLABS, OWN + plan.frame_rows, LANES), F32),
            pltpu.VMEM((tokens + 8, MIXED), F32),
            pltpu.VMEM((STATE, OWN), F32),
            pltpu.SemaphoreType.DMA((dp + 2 * GROUP,)),
        ],
        name="forward",
        **params_of(8e9, 3e7, limit),
    )(place, sc, tok, segr, *x_pieces, *c_pieces, *weights)
    proj, ssd, d_gated, states, sums, w_in, w_out, small, normed, x_hat, cots = forward
    near, far, both = [swap(sums, "seq", r) for r in range(1, GROUP)]
    sums = (sums + near) + (far + both)

    backward = pl.pallas_call(
        functools.partial(backward_kernel, plan),
        out_shape=[shape((GROUP, block, LANES), BF16)] * dp
        + [shape((2, 2, piece, D), BF16)] * 2,
        in_specs=[smem_spec(), smem_spec()] + [vmem_spec()] * 13,
        out_specs=[any_spec()] * dp + [vmem_spec()] * 2,
        scratch_shapes=[
            pltpu.VMEM((dp, GROUP, block, LANES), BF16),
            pltpu.VMEM((tokens + 8, MIXED), F32),
            pltpu.VMEM((tokens + 8, MIXED), F32),
            pltpu.VMEM((STATE, OWN), F32),
            pltpu.VMEM((tokens, OWN), BF16),
            pltpu.VMEM((tokens, WIDE), BF16),
            pltpu.VMEM((CHUNK, LANES), F32),
            pltpu.VMEM((8, OWN), F32),
            pltpu.VMEM((8, OWN), F32),
            pltpu.VMEM((8 * (KERNEL + 1), MIXED), F32),
            pltpu.VMEM((16, LANES), F32),
            pltpu.VMEM((8, D), F32),
            pltpu.VMEM((SLABS, D + plan.pure, LANES), F32),
            pltpu.VMEM((OUT_SLABS, OWN + plan.frame_rows, LANES), F32),
            pltpu.SemaphoreType.DMA((dp,)),
        ],
        name="backward",
        **params_of(16e9, 4e7, limit),
    )(place, sc, tok, segr, sums, proj, ssd, d_gated, states, w_in, w_out, small, normed,
      x_hat, cots)
    terms, act_terms, back_terms = backward[:dp], backward[dp], backward[dp + 1]

    def joined(a, b):
        return (a.astype(F32) + b.astype(F32)).astype(BF16)

    def column(j):
        return joined(terms[2 * j], swap(terms[2 * j + 1], "dp", 1))

    moving = None
    for j in range(line - 1, 0, -1):
        here = column(j)
        moving = along(here if moving is None else joined(here, moving))
    here = column(0)
    reduced = here if moving is None else joined(here, moving)
    blocks = exchange(reduced)

    flat_shape = shape((sublanes, LANES), F32)
    updated = pl.pallas_call(
        functools.partial(unpack_kernel, plan),
        out_shape=[flat_shape] * 4,
        in_specs=[smem_spec()] + [vmem_spec()] * 4,
        out_specs=[vmem_spec()] * 4,
        scratch_shapes=[
            pltpu.VMEM((scratch_rows, LANES), F32),
            pltpu.VMEM((plan.pure * ROW_SLABS, LANES), F32),
            pltpu.VMEM((plan.frame, LANES), F32),
        ],
        name="unpack",
        **params_of(1e6, 5e6),
    )(
        where,
        blocks,
        flat_params,
        moment_one.reshape(sublanes, LANES),
        moment_two.reshape(sublanes, LANES),
    )
    grad, new_params, new_one, new_two = [value.reshape(length) for value in updated]

    residual = inputs[0]
    activation = residual + sum_pieces(act_terms)
    d_normed = sum_pieces(back_terms)
    inv_rms = lax.rsqrt(jnp.mean(residual * residual, axis=-1, keepdims=True) + NORM_EPS)
    hat = residual * inv_rms
    norm_gain = small[25:31].reshape(D)
    d_hat = d_normed * norm_gain
    d_front = inv_rms * (d_hat - hat * jnp.mean(d_hat * hat, axis=-1, keepdims=True))
    gradient = out_grad[0] + d_front
    return (activation[None], gradient[None], grad, new_params, new_one, new_two)


def solution(mesh):
    tokens = P("dp", "seq", None)
    flat = P(("dp", "seq"))

    return jax.shard_map(
        local,
        mesh=mesh,
        in_specs=(tokens, tokens, P("dp", None), flat, flat, flat),
        out_specs=(tokens, tokens, flat, flat, flat, flat),
        check_vma=False,
    )
```
